32 devices in a mesh: groups: 2 (over x), seq: 16 (over z, y, core).
Axes of the slice: x: 2, y: 2, z: 4, core: 2. Of those that a mesh axis runs over, the one named last changes fastest.
Arguments:
- target_queries: bfloat16 [16384, 1024], P(('groups', 'seq')), parts along dimension 0, may hold values from -8 to 8
- memory_keys: bfloat16 [16384, 1024], P(('groups', 'seq')), parts along dimension 0, may hold values from -8 to 8
- memory_values: bfloat16 [16384, 1024], P(('groups', 'seq')), parts along dimension 0, may hold values from -6 to 6
- grad_output: bfloat16 [16384, 1024], P(('groups', 'seq')), parts along dimension 0, may hold values from -6 to 6
- band_start: int32 [128], P(('groups', 'seq')), parts along dimension 0, may hold values from 0 to 63, as said below
- band_end: int32 [128], P(('groups', 'seq')), parts along dimension 0, may hold values from 4 to 64, as said below
Outputs:
- attended: bfloat16 [16384, 1024], P(('groups', 'seq')), parts along dimension 0
- grad_queries: bfloat16 [16384, 1024], P(('groups', 'seq')), parts along dimension 0
- grad_keys: bfloat16 [16384, 1024], P(('groups', 'seq')), parts along dimension 0
- grad_values: bfloat16 [16384, 1024], P(('groups', 'seq')), parts along dimension 0
The draws below stay inside these ranges and needn't reach their ends.
There are 2 independent parts, one for each index of `groups`. The reference program is written for one: setup_inputs(seed, part) draws one part's arguments, and reference() takes and returns one part's arrays. A program takes and returns all parts, laid end to end along the dimension named above; each array names one. Nothing has to cross between parts.
Inputs may be any that keep to these rules, and one draw needn't show every extreme that they name: band_start never falls as the target block b grows, and band_start[b] lies between b - 3 and b. band_end never falls as b grows, and band_end[b] - band_start[b] lies between 1 and 4; the difference 4 occurs in every draw.
All inputs are finite; a program needn't handle non-finite values.
Results may differ from the reference program's by a relative error of at most 0.024.
Values may be sent and summed in bfloat16 or wider, within the bound.
No kernel may reach another device: no remote copies, remote signals or barrier semaphores. Data moves between devices by JAX's collectives and lax.ppermute only.
A program may use at most 128 MiB of HBM per device.

```python
import math
import jax
import jax.numpy as jnp
from jax import lax

D = 1024
H = 16
BLOCK = 128
MAX_BAND = 4
NBLOCKS = 64
TOKENS = 8192
N_SEQ = 16


def band_tables(key):
    base_key = jax.random.fold_in(key, 7001)
    back_key, span_key = jax.random.split(base_key)
    blocks = jnp.arange(NBLOCKS, dtype=jnp.int32)
    backward = jax.random.randint(back_key, (NBLOCKS,), 0, MAX_BAND, dtype=jnp.int32)
    backward = backward.at[NBLOCKS - 1].set(0)
    first_band = jnp.clip(lax.cummax(blocks - backward, axis=0), 0, NBLOCKS - 1)
    spans = jax.random.randint(span_key, (NBLOCKS,), 1, MAX_BAND + 1, dtype=jnp.int32)
    spans = spans.at[0].set(MAX_BAND)
    spans = spans.at[NBLOCKS - 1].set(MAX_BAND)
    last_band = jnp.minimum(lax.cummax(first_band + spans, axis=0), NBLOCKS)
    return (first_band.astype(jnp.int32), last_band.astype(jnp.int32))


def draw_band_start(key, part):
    return band_tables(key)[0]


def draw_band_end(key, part):
    return band_tables(key)[1]


def draw_target_queries(key, part):
    noise = jax.random.normal(jax.random.fold_in(key, 11), (TOKENS, D), jnp.float32)
    noise = jnp.clip(noise, -6.0, 6.0)
    return noise.astype(jnp.bfloat16)


def draw_memory_keys(key, part):
    noise = jax.random.normal(jax.random.fold_in(key, 21), (TOKENS, D), jnp.float32)
    noise = jnp.clip(noise, -6.0, 6.0)
    return noise.astype(jnp.bfloat16)


def block_scale(key, dims, pieces, low, high):
    gain, own = 1.0, jax.random.fold_in(key, 6)
    for dim, blocks in pieces:
        steps = jnp.exp(jax.random.uniform(jax.random.fold_in(own, dim), (blocks,), jnp.float32, low / len(pieces), high / len(pieces)))
        gain = gain * jnp.repeat(steps, dims[dim] // blocks).reshape([-1 if axis == dim else 1 for axis in range(len(dims))])
    return gain


def scatter_about(stream_key, shape, scale, reach, shards=(), kind=jnp.bfloat16):
    gain = block_scale(stream_key, shape, shards, -0.22, 0.18) if shards else 1.0
    entries = jax.random.normal(stream_key, shape, jnp.float32) * scale * gain
    return jnp.minimum(jnp.maximum(entries, -reach), reach).astype(kind)


def setup_inputs(seed: int = 0, part: int = 0) -> dict:
    seeds = jax.random.split(jax.random.key(seed), 7)
    part_keys = jax.random.split(jax.random.fold_in(seeds[6], part), 7)
    target_queries = draw_target_queries(jax.random.fold_in(jax.random.fold_in(seeds[6], part), 71), part)
    memory_keys = draw_memory_keys(jax.random.fold_in(jax.random.fold_in(seeds[6], part), 71), part)
    memory_values = scatter_about(part_keys[2], (TOKENS, D), 1.0, 6.0, ((0, 16),))
    grad_output = scatter_about(part_keys[3], (TOKENS, D), 1.0, 6.0, ((0, 16),))
    band_start = draw_band_start(jax.random.fold_in(jax.random.fold_in(seeds[6], part), 71), part)
    band_end = draw_band_end(jax.random.fold_in(jax.random.fold_in(seeds[6], part), 71), part)
    return {"target_queries": target_queries, "memory_keys": memory_keys, "memory_values": memory_values, "grad_output": grad_output, "band_start": band_start, "band_end": band_end}


def reference(target_queries, memory_keys, memory_values, grad_output, band_start, band_end):
    total_rows, model_width = target_queries.shape
    block_count = total_rows // BLOCK
    head_dim = model_width // H
    span_rows = MAX_BAND * BLOCK
    reach_rows = (MAX_BAND - 1) * BLOCK
    dev_blocks = block_count // N_SEQ
    shard_rows = dev_blocks * BLOCK
    local_rows = shard_rows + 2 * reach_rows
    score_scale = 1.0 / math.sqrt(head_dim)
    padding = jnp.zeros((span_rows, model_width), target_queries.dtype)
    key_padded = jnp.concatenate([memory_keys, padding], axis=0)
    value_padded = jnp.concatenate([memory_values, padding], axis=0)
    query_blocks = target_queries.reshape(N_SEQ, dev_blocks, BLOCK, model_width)
    grad_blocks = grad_output.reshape(N_SEQ, dev_blocks, BLOCK, model_width)
    start_runs = band_start.reshape(N_SEQ, dev_blocks)
    end_runs = band_end.reshape(N_SEQ, dev_blocks)
    column_block = jnp.arange(span_rows, dtype=jnp.int32) // BLOCK

    def one_device(totals, device_inputs):
        dev_index, query_run, grad_run, start_run, end_run = device_inputs

        def one_block(local, inputs):
            query_rows, grad_rows, first_band, last_band = inputs
            row_first = (first_band * BLOCK).astype(jnp.int32)
            local_first = ((first_band - dev_index * dev_blocks) * BLOCK + reach_rows).astype(jnp.int32)
            key_rows = lax.dynamic_slice_in_dim(key_padded, row_first, span_rows, 0)
            value_rows = lax.dynamic_slice_in_dim(value_padded, row_first, span_rows, 0)
            query_heads = query_rows.astype(jnp.float32).reshape(BLOCK, H, head_dim)
            grad_heads = grad_rows.astype(jnp.float32).reshape(BLOCK, H, head_dim)
            key_heads = key_rows.astype(jnp.float32).reshape(span_rows, H, head_dim)
            value_heads = value_rows.astype(jnp.float32).reshape(span_rows, H, head_dim)
            scores = jnp.einsum('qhd,khd->hqk', query_heads, key_heads) * score_scale
            allowed = column_block < last_band - first_band
            scores = jnp.where(allowed[None, None, :], scores, -1e+30)
            row_max = lax.optimization_barrier(jnp.max(scores, axis=-1, keepdims=True))
            weights = jnp.exp(scores - row_max)
            probs = weights / lax.optimization_barrier(jnp.sum(weights, axis=-1, keepdims=True))
            probs_low = lax.optimization_barrier(probs.astype(jnp.bfloat16)).astype(jnp.float32)
            attended = jnp.einsum('hqk,khd->qhd', probs_low, value_heads)
            attended_low = lax.optimization_barrier(attended.astype(jnp.bfloat16))
            row_dot = jnp.einsum('qhd,qhd->hq', grad_heads, attended_low.astype(jnp.float32))
            grad_probs = jnp.einsum('qhd,khd->hqk', grad_heads, value_heads)
            grad_scores = probs * (grad_probs - row_dot[:, :, None])
            grad_scores = lax.optimization_barrier(grad_scores.astype(jnp.bfloat16)).astype(jnp.float32)
            grad_query = (jnp.einsum('hqk,khd->qhd', grad_scores, key_heads) * score_scale).astype(jnp.bfloat16)
            grad_key = jnp.einsum('hqk,qhd->khd', grad_scores, query_heads) * score_scale
            grad_value = jnp.einsum('hqk,qhd->khd', probs_low, grad_heads)
            update = jnp.stack([grad_key.reshape(span_rows, model_width), grad_value.reshape(span_rows, model_width)])
            corner = (jnp.int32(0), local_first, jnp.int32(0))
            current = lax.dynamic_slice(local, corner, (2, span_rows, model_width))
            local = lax.dynamic_update_slice(local, current + update, corner)
            return (local, (attended_low.reshape(BLOCK, model_width), grad_query.reshape(BLOCK, model_width)))
        local = jnp.zeros((2, local_rows, model_width), jnp.float32)
        local, outputs = lax.scan(one_block, local, (query_run, grad_run, start_run, end_run))
        lower = lax.optimization_barrier(local[:, :reach_rows].astype(jnp.bfloat16)).astype(jnp.float32)
        upper = lax.optimization_barrier(local[:, reach_rows + shard_rows:].astype(jnp.bfloat16)).astype(jnp.float32)
        middle = local[:, reach_rows:reach_rows + shard_rows]
        rounded = jnp.concatenate([lower, middle, upper], axis=1)
        corner = (jnp.int32(0), (dev_index * shard_rows).astype(jnp.int32), jnp.int32(0))
        current = lax.dynamic_slice(totals, corner, (2, local_rows, model_width))
        totals = lax.dynamic_update_slice(totals, current + rounded, corner)
        return (totals, outputs)
    totals = jnp.zeros((2, total_rows + 2 * reach_rows, model_width), jnp.float32)
    device_ids = jnp.arange(N_SEQ, dtype=jnp.int32)
    totals, (attended_all, grad_query_all) = lax.scan(one_device, totals, (device_ids, query_blocks, grad_blocks, start_runs, end_runs))
    attended_out = attended_all.reshape(total_rows, model_width)
    grad_queries = grad_query_all.reshape(total_rows, model_width)
    grad_keys = totals[0, reach_rows:reach_rows + total_rows].astype(jnp.bfloat16)
    grad_values = totals[1, reach_rows:reach_rows + total_rows].astype(jnp.bfloat16)
    return (attended_out, grad_queries, grad_keys, grad_values)
```

```python
import functools
import math

import jax
import jax.numpy as jnp
from jax import lax
from jax.experimental import pallas as pl
from jax.experimental.pallas import tpu as pltpu
from jax.sharding import PartitionSpec as P

H = 16
BLOCK = 128
MAX_BAND = 4
REACH = MAX_BAND - 1
SLOTS = 2
HEADER = 16
PIECES = 2
VMEM_LIMIT = 48 * 1024 * 1024

ANY = pl.BlockSpec(memory_space=pl.ANY)
SMEM = pl.BlockSpec(memory_space=pltpu.SMEM)


def rows(block, count=1):
    if isinstance(block, int):
        return pl.ds(block * BLOCK, count * BLOCK)
    return pl.ds(pl.multiple_of(block * BLOCK, BLOCK), count * BLOCK)


def run_copies(copies):
    for copy in copies:
        copy.start()
    for copy in copies:
        copy.wait()


def moved_up(starts, ends, first, blocks):
    return ends[blocks - 1] == first + blocks + REACH


def moved_down(starts, ends, first):
    return starts[0] == first - REACH


def pack_kernel(blocks, piece, width, header, starts, ends, place, q, k, v, g, inter, intra, head, sem):
    first, odd = place[0], place[1]
    up = moved_up(starts, ends, first, blocks)
    down = moved_down(starts, ends, first)
    cols = pl.ds(piece * width, width)

    def send(message, edge, behind, moves, value, slot):
        def copy(source, block, index):
            return pltpu.make_async_copy(
                source.at[rows(block), cols], message.at[rows(index)], sem.at[slot * 5 + index]
            )

        near = [copy(k, edge, 0), copy(v, edge, 1)]
        target = [copy(q, edge, 2), copy(g, edge, 3)]
        far = [copy(k, behind, 2), copy(v, behind, 3)]
        for c in near:
            c.start()

        @pl.when(moves)
        def _():
            for c in target:
                c.start()

        @pl.when(jnp.logical_not(moves))
        def _():
            for c in far:
                c.start()

        waits = near + far
        if header:
            head[slot] = jnp.full((HEADER, width), value.astype(jnp.float32)).astype(head.dtype)
            tail = pltpu.make_async_copy(
                head.at[slot], message.at[pl.ds(2 * SLOTS * BLOCK, HEADER)], sem.at[slot * 5 + 4]
            )
            tail.start()
            waits = waits + [tail]
        return waits

    up_value = jnp.where(up, MAX_BAND, 0)
    down_value = jnp.where(down, ends[0] - starts[0], 0)
    is_odd = odd == 1
    edge = jnp.where(is_odd, blocks - 1, 0)
    behind = jnp.where(is_odd, blocks - 2, 1)
    moves = jnp.where(is_odd, up.astype(jnp.int32), down.astype(jnp.int32)) == 1
    value = jnp.where(is_odd, up_value, down_value)
    waits = send(inter, edge, behind, moves, value, 0)
    edge = jnp.where(is_odd, 0, blocks - 1)
    behind = jnp.where(is_odd, 1, blocks - 2)
    moves = jnp.where(is_odd, down.astype(jnp.int32), up.astype(jnp.int32)) == 1
    value = jnp.where(is_odd, down_value, up_value)
    waits += send(intra, edge, behind, moves, value, 1)
    for c in waits:
        c.wait()


def pack(blocks, piece, width, starts, ends, place, q, k, v, g):
    header = piece == 0
    shape = jax.ShapeDtypeStruct((2 * SLOTS * BLOCK + (HEADER if header else 0), width), q.dtype)
    return pl.pallas_call(
        functools.partial(pack_kernel, blocks, piece, width, header),
        out_shape=(shape, shape),
        in_specs=[SMEM] * 3 + [ANY] * 4,
        out_specs=(ANY, ANY),
        scratch_shapes=[
            pltpu.VMEM((2, HEADER, width), q.dtype),
            pltpu.SemaphoreType.DMA((10,)),
        ],
        name=f"pack{piece}",
    )(starts, ends, place, q, k, v, g)


def attend_pair(count, head_dim, q_row, k_row, lane, kb, vb, qb, gb, dk, dv, ob, dqb):
    dtype = kb.dtype
    lanes = pl.ds(lane, 2 * head_dim)
    window = pl.ds(k_row, count * BLOCK)
    left = lax.broadcasted_iota(jnp.int32, (BLOCK, 2 * head_dim), 1) < head_dim
    zero = jnp.zeros((BLOCK, 2 * head_dim), dtype)
    q = qb[pl.ds(q_row, BLOCK), lanes] * jnp.asarray(1.0 / math.sqrt(head_dim), dtype)
    g = gb[pl.ds(q_row, BLOCK), lanes]
    q = jnp.concatenate([jnp.where(left, q, zero), jnp.where(left, zero, q)], axis=0)
    g = jnp.concatenate([jnp.where(left, g, zero), jnp.where(left, zero, g)], axis=0)
    keys = kb[window, lanes]
    values = vb[window, lanes]
    by_row = (((1,), (1,)), ((), ()))
    by_key = (((0,), (0,)), ((), ()))
    plain = (((1,), (0,)), ((), ()))
    dot = functools.partial(lax.dot_general, preferred_element_type=jnp.float32)
    scores = dot(keys, q, by_row)
    top = jnp.max(scores, axis=0, keepdims=True)
    weights = jnp.exp(scores - top)
    grad_probs = dot(values, g, by_row)
    scale = 1.0 / jnp.sum(weights, axis=0, keepdims=True)
    row_dot = jnp.sum(weights * grad_probs, axis=0, keepdims=True) * scale
    probs = weights * scale
    low = probs.astype(dtype)
    grad_scores = (probs * (grad_probs - row_dot)).astype(dtype)
    dv[window, lanes] += dot(low, g, plain)
    dk[window, lanes] += dot(grad_scores, q, plain)
    out = dot(values, low, by_key)
    grad_q = dot(keys, grad_scores, by_key) * (1.0 / math.sqrt(head_dim))

    def diagonal(x):
        return jnp.concatenate([x[:head_dim, :BLOCK], x[head_dim:, BLOCK:]], axis=0).T.astype(dtype)

    ob[pl.ds(q_row, BLOCK), lanes] = diagonal(out)
    dqb[pl.ds(q_row, BLOCK), lanes] = diagonal(grad_q)


def attend_kernel(
    blocks, piece, width, head_dim,
    starts, ends, place, q, k, v, g, inter, intra, inter_head, intra_head, *rest
):
    if piece:
        rest = rest[2:]
    attended, grad_q, back_inter, back_intra, grad_k, grad_v = rest[:6]
    kb, vb, qb, gb, dk, dv, ob, dqb, low, head, sem = rest[6:]
    first, odd = place[0], place[1]
    cols = pl.ds(piece * width, width)
    own = rows(SLOTS, blocks)
    count = [0]

    def copy(source, target):
        count[0] += 1
        return pltpu.make_async_copy(source, target, sem.at[count[0] - 1])

    heads = [
        copy(inter_head.at[pl.ds(2 * SLOTS * BLOCK, HEADER)], head.at[0]),
        copy(intra_head.at[pl.ds(2 * SLOTS * BLOCK, HEADER)], head.at[1]),
    ]
    loads = [
        copy(k.at[:, cols], kb.at[own]),
        copy(v.at[:, cols], vb.at[own]),
        copy(q.at[:, cols], qb.at[rows(1, blocks)]),
        copy(g.at[:, cols], gb.at[rows(1, blocks)]),
    ]
    for c in heads + loads:
        c.start()
    is_odd = odd == 1
    for c in heads:
        c.wait()
    from_inter = jnp.max(head[0].astype(jnp.float32)).astype(jnp.int32)
    from_intra = jnp.max(head[1].astype(jnp.float32)).astype(jnp.int32)
    below_span = jnp.where(is_odd, from_intra, from_inter)
    above_span = jnp.where(is_odd, from_inter, from_intra)

    near_below, far_below = SLOTS - 1, SLOTS - 2
    near_above, far_above = SLOTS + blocks, SLOTS + blocks + 1
    base = count[0]

    def arrive(message, near, far, target, span, slot):
        at = lambda i: sem.at[base + slot * 4 + i]
        part = lambda i: message.at[rows(i)]
        make = pltpu.make_async_copy
        always = [make(part(0), kb.at[rows(near)], at(0)), make(part(1), vb.at[rows(near)], at(1))]
        moved = [make(part(2), qb.at[rows(target)], at(2)), make(part(3), gb.at[rows(target)], at(3))]
        stays = [make(part(2), kb.at[rows(far)], at(2)), make(part(3), vb.at[rows(far)], at(3))]
        for c in always:
            c.start()

        @pl.when(span > 0)
        def _():
            for c in moved:
                c.start()

        @pl.when(span == 0)
        def _():
            for c in stays:
                c.start()

        return always + stays

    inter_near = jnp.where(is_odd, near_above, near_below)
    inter_far = jnp.where(is_odd, far_above, far_below)
    inter_target = jnp.where(is_odd, blocks + 1, 0)
    intra_near = jnp.where(is_odd, near_below, near_above)
    intra_far = jnp.where(is_odd, far_below, far_above)
    intra_target = jnp.where(is_odd, 0, blocks + 1)
    loads += arrive(inter, inter_near, inter_far, inter_target, from_inter, 0)
    loads += arrive(intra, intra_near, intra_far, intra_target, from_intra, 1)
    dk[...] = jnp.zeros_like(dk)
    dv[...] = jnp.zeros_like(dv)
    for c in loads:
        c.wait()

    up = moved_up(starts, ends, first, blocks)
    down = moved_down(starts, ends, first)

    def task(index, carry):
        mine = jnp.clip(index - 1, 0, blocks - 1)
        lower, upper = index == 0, index == blocks + 1
        span = ends[mine] - starts[mine]
        gone = ((index == 1) & down) | ((index == blocks) & up)
        span = jnp.where(gone, 0, span)
        span = jnp.where(lower, below_span, jnp.where(upper, above_span, span))
        window = starts[mine] - first + SLOTS
        window = jnp.where(lower, near_below, jnp.where(upper, near_above - REACH, window))
        q_row = pl.multiple_of(index * BLOCK, BLOCK)
        k_row = pl.multiple_of(window * BLOCK, BLOCK)
        for size in range(1, MAX_BAND + 1):

            @pl.when(span == size)
            def _():
                @pl.loop(0, width // (2 * head_dim))
                def _(pair):
                    lane = pl.multiple_of(pair * 2 * head_dim, 2 * head_dim)
                    attend_pair(size, head_dim, q_row, k_row, lane, kb, vb, qb, gb, dk, dv, ob, dqb)

        return carry

    lax.fori_loop(0, blocks + 2, task, 0)

    stores = [
        (ob.at[rows(1, blocks)], attended.at[:, cols]),
        (dqb.at[rows(1, blocks)], grad_q.at[:, cols]),
        (dk.at[own], grad_k),
        (dv.at[own], grad_v),
    ]
    stores = [pltpu.make_async_copy(a, b, sem.at[i]) for i, (a, b) in enumerate(stores)]
    for c in stores:
        c.start()

    def leave(message, near, far, target, span, slot):
        at = lambda i: sem.at[base + slot * 2 + i]
        low[slot, rows(0)] = dk[rows(near)].astype(low.dtype)
        low[slot, rows(1)] = dv[rows(near)].astype(low.dtype)

        @pl.when(span > 0)
        def _():
            low[slot, rows(2)] = ob[rows(target)]
            low[slot, rows(3)] = dqb[rows(target)]

        @pl.when(span == 0)
        def _():
            low[slot, rows(2)] = dk[rows(far)].astype(low.dtype)
            low[slot, rows(3)] = dv[rows(far)].astype(low.dtype)

        c = pltpu.make_async_copy(low.at[slot], message, at(0))
        c.start()
        return [c]

    stores += leave(back_inter, inter_near, inter_far, inter_target, from_inter, 0)
    stores += leave(back_intra, intra_near, intra_far, intra_target, from_intra, 1)
    for c in stores:
        c.wait()


def attend(blocks, piece, width, head_dim, starts, ends, place, q, k, v, g, inter, intra, heads, outs):
    low, high = q.dtype, jnp.float32
    back = jax.ShapeDtypeStruct((2 * SLOTS * BLOCK, width), low)
    whole = jax.ShapeDtypeStruct(q.shape, low)
    total = jax.ShapeDtypeStruct((blocks * BLOCK, width), high)
    sources, targets = (blocks + 2 * SLOTS) * BLOCK, (blocks + 2) * BLOCK
    pairs = blocks * MAX_BAND * (width // (2 * head_dim))
    return pl.pallas_call(
        functools.partial(attend_kernel, blocks, piece, width, head_dim),
        out_shape=(whole, whole, back, back, total, total),
        in_specs=[SMEM] * 3 + [ANY] * (8 + len(outs)),
        out_specs=(ANY,) * 6,
        input_output_aliases={11: 0, 12: 1} if outs else {},
        scratch_shapes=[
            pltpu.VMEM((sources, width), low),
            pltpu.VMEM((sources, width), low),
            pltpu.VMEM((targets, width), low),
            pltpu.VMEM((targets, width), low),
            pltpu.VMEM((sources, width), high),
            pltpu.VMEM((sources, width), high),
            pltpu.VMEM((targets, width), low),
            pltpu.VMEM((targets, width), low),
            pltpu.VMEM((2, 2 * SLOTS * BLOCK, width), low),
            pltpu.VMEM((2, HEADER, width), low),
            pltpu.SemaphoreType.DMA((14,)),
        ],
        compiler_params=pltpu.CompilerParams(vmem_limit_bytes=VMEM_LIMIT),
        cost_estimate=pl.CostEstimate(
            flops=pairs * 12 * BLOCK * 2 * BLOCK * BLOCK, transcendentals=pairs * 2 * BLOCK * BLOCK,
            bytes_accessed=16 * blocks * BLOCK * width,
        ),
        name=f"attend{piece}",
    )(starts, ends, place, q, k, v, g, inter, intra, *heads, *outs)


def settle_kernel(
    blocks, piece, width, starts, ends, place, grad_k, grad_v, inter, intra, *rest
):
    rest = rest[4:] if piece else rest[2:]
    attended, grad_q, out_k, out_v = rest[:4]
    above, below, stage, sem = rest[4:]
    first, odd = place[0], place[1]
    cols = pl.ds(piece * width, width)
    up = moved_up(starts, ends, first, blocks)
    down = moved_down(starts, ends, first)
    is_odd = odd == 1

    @pl.when(is_odd)
    def _():
        run_copies([
            pltpu.make_async_copy(inter, above, sem.at[0]),
            pltpu.make_async_copy(intra, below, sem.at[1]),
        ])

    @pl.when(jnp.logical_not(is_odd))
    def _():
        run_copies([
            pltpu.make_async_copy(intra, above, sem.at[0]),
            pltpu.make_async_copy(inter, below, sem.at[1]),
        ])

    last = blocks - 1
    high = jnp.float32
    keep_up = jnp.logical_not(up)
    keep_down = jnp.logical_not(down)
    for i, (total, stored) in enumerate(((grad_k, stage.at[0]), (grad_v, stage.at[1]))):
        for block in range(blocks):
            value = total[rows(block)]
            if block == 0:
                value += below[rows(i)].astype(high)
            if block == 1:
                far = below[rows(2 + i)].astype(high)
                value += jnp.where(keep_down, far, jnp.zeros_like(far))
            if block == last:
                value += above[rows(i)].astype(high)
            if block == last - 1:
                far = above[rows(2 + i)].astype(high)
                value += jnp.where(keep_up, far, jnp.zeros_like(far))
            stored[rows(block)] = value.astype(stage.dtype)
    stores = [
        pltpu.make_async_copy(stage.at[0], out_k.at[:, cols], sem.at[0]),
        pltpu.make_async_copy(stage.at[1], out_v.at[:, cols], sem.at[1]),
    ]
    for c in stores:
        c.start()

    @pl.when(up)
    def _():
        run_copies([
            pltpu.make_async_copy(above.at[rows(2)], attended.at[rows(last), cols], sem.at[2]),
            pltpu.make_async_copy(above.at[rows(3)], grad_q.at[rows(last), cols], sem.at[3]),
        ])

    @pl.when(down)
    def _():
        run_copies([
            pltpu.make_async_copy(below.at[rows(2)], attended.at[rows(0), cols], sem.at[2]),
            pltpu.make_async_copy(below.at[rows(3)], grad_q.at[rows(0), cols], sem.at[3]),
        ])

    for c in stores:
        c.wait()


def settle(blocks, piece, width, starts, ends, place, grad_k, grad_v, inter, intra, attended, grad_q, outs):
    low = attended.dtype
    whole = jax.ShapeDtypeStruct(attended.shape, low)
    message = 2 * SLOTS * BLOCK
    vmem = pl.BlockSpec(memory_space=pltpu.VMEM)
    aliases = {7: 0, 8: 1}
    if outs:
        aliases.update({9: 2, 10: 3})
    return pl.pallas_call(
        functools.partial(settle_kernel, blocks, piece, width),
        out_shape=(whole,) * 4,
        in_specs=[SMEM] * 3 + [vmem] * 2 + [ANY] * (4 + len(outs)),
        out_specs=(ANY,) * 4,
        input_output_aliases=aliases,
        scratch_shapes=[
            pltpu.VMEM((message, width), low),
            pltpu.VMEM((message, width), low),
            pltpu.VMEM((2, blocks * BLOCK, width), low),
            pltpu.SemaphoreType.DMA((4,)),
        ],
        compiler_params=pltpu.CompilerParams(vmem_limit_bytes=VMEM_LIMIT),
        name=f"settle{piece}",
    )(starts, ends, place, grad_k, grad_v, inter, intra, attended, grad_q, *outs)


def body(q, k, v, g, starts, ends):
    shard_rows, model_width = q.shape
    blocks = shard_rows // BLOCK
    head_dim = model_width // H
    width = model_width // PIECES
    count = lax.axis_size("seq")
    index = lax.axis_index("seq")
    place = jnp.stack([index * blocks, index % 2]).astype(jnp.int32)
    across = [(i, i + 1) for i in range(1, count - 1, 2)] + [(i + 1, i) for i in range(1, count - 1, 2)]
    inside = [(i, i ^ 1) for i in range(count)]
    swap = lambda inter, intra: (lax.ppermute(inter, "seq", across), lax.ppermute(intra, "seq", inside))

    arrived = []
    for piece in range(PIECES):
        arrived.append(swap(*pack(blocks, piece, width, starts, ends, place, q, k, v, g)))
    heads = arrived[0]
    outs, totals, returned = (), [], []
    for piece in range(PIECES):
        results = attend(
            blocks, piece, width, head_dim, starts, ends, place, q, k, v, g, *arrived[piece], heads, outs
        )
        outs = results[:2]
        returned.append(swap(*results[2:4]))
        totals.append(results[4:])
    attended, grad_q = outs
    outs = ()
    for piece in range(PIECES):
        attended, grad_q, *outs = settle(
            blocks, piece, width, starts, ends, place, *totals[piece], *returned[piece], attended, grad_q, outs
        )
    return (attended, grad_q, *outs)


def solution(mesh):
    spec = P(("groups", "seq"), None)
    flat = P(("groups", "seq"))
    return jax.shard_map(
        body,
        mesh=mesh,
        in_specs=(spec, spec, spec, spec, flat, flat),
        out_specs=(spec, spec, spec, spec),
        check_vma=False,
    )
```

```python
import functools
import math

import jax
import jax.numpy as jnp
from jax import lax
from jax.experimental import pallas as pl
from jax.experimental.pallas import tpu as pltpu
from jax.sharding import PartitionSpec as P

H = 16
BLOCK = 128
MAX_BAND = 4
REACH = MAX_BAND - 1
SLOTS = 2
HEADER = 16
PIECES = 2
VMEM_LIMIT = 48 * 1024 * 1024

ANY = pl.BlockSpec(memory_space=pl.ANY)
SMEM = pl.BlockSpec(memory_space=pltpu.SMEM)


def rows(block, count=1):
    if isinstance(block, int):
        return pl.ds(block * BLOCK, count * BLOCK)
    return pl.ds(pl.multiple_of(block * BLOCK, BLOCK), count * BLOCK)


def run_copies(copies):
    for copy in copies:
        copy.start()
    for copy in copies:
        copy.wait()


def moved_up(starts, ends, first, blocks):
    return ends[blocks - 1] == first + blocks + REACH


def moved_down(starts, ends, first):
    return starts[0] == first - REACH


def pack_kernel(blocks, piece, width, header, starts, ends, place, q, k, v, g, inter, intra, stage, sem):
    first, odd = place[0], place[1]
    up = moved_up(starts, ends, first, blocks)
    down = moved_down(starts, ends, first)
    cols = pl.ds(piece * width, width)
    make = pltpu.make_async_copy

    def gather(edge, behind, moves, slot):
        def copy(source, block, index):
            return make(source.at[rows(block), cols], stage.at[slot, rows(index)], sem.at[slot * 5 + index])

        near = [copy(k, edge, 0), copy(v, edge, 1)]
        target = [copy(q, edge, 2), copy(g, edge, 3)]
        far = [copy(k, behind, 2), copy(v, behind, 3)]
        for c in near:
            c.start()

        @pl.when(moves)
        def _():
            for c in target:
                c.start()

        @pl.when(jnp.logical_not(moves))
        def _():
            for c in far:
                c.start()

        return near + far

    up_value = jnp.where(up, MAX_BAND, 0)
    down_value = jnp.where(down, ends[0] - starts[0], 0)
    is_odd = odd == 1
    moves_up = (is_odd & up) | (jnp.logical_not(is_odd) & down)
    moves_down = (is_odd & down) | (jnp.logical_not(is_odd) & up)
    waits = (
        gather(jnp.where(is_odd, blocks - 1, 0), jnp.where(is_odd, blocks - 2, 1), moves_up, 0),
        gather(jnp.where(is_odd, 0, blocks - 1), jnp.where(is_odd, 1, blocks - 2), moves_down, 1),
    )
    values = (jnp.where(is_odd, up_value, down_value), jnp.where(is_odd, down_value, up_value))
    sends = []
    for slot, (message, value) in enumerate(zip((inter, intra), values)):
        if header:
            stage[slot, pl.ds(2 * SLOTS * BLOCK, HEADER)] = jnp.full(
                (HEADER, width), value.astype(jnp.float32)
            ).astype(stage.dtype)
        for c in waits[slot]:
            c.wait()
        sends.append(make(stage.at[slot], message, sem.at[slot * 5 + 4]))
        sends[-1].start()
    for c in sends:
        c.wait()


def pack(blocks, piece, width, starts, ends, place, q, k, v, g):
    header = piece == 0
    shape = jax.ShapeDtypeStruct((2 * SLOTS * BLOCK + (HEADER if header else 0), width), q.dtype)
    return pl.pallas_call(
        functools.partial(pack_kernel, blocks, piece, width, header),
        out_shape=(shape, shape),
        in_specs=[SMEM] * 3 + [ANY] * 4,
        out_specs=(ANY, ANY),
        scratch_shapes=[
            pltpu.VMEM((2, *shape.shape), q.dtype),
            pltpu.SemaphoreType.DMA((10,)),
        ],
        name=f"pack{piece}",
    )(starts, ends, place, q, k, v, g)


def attend_pair(count, head_dim, q_row, k_row, lane, kb, vb, qb, gb, dk, dv, ob, dqb):
    dtype = kb.dtype
    lanes = pl.ds(lane, 2 * head_dim)
    window = pl.ds(k_row, count * BLOCK)
    left = lax.broadcasted_iota(jnp.int32, (BLOCK, 2 * head_dim), 1) < head_dim
    zero = jnp.zeros((BLOCK, 2 * head_dim), dtype)
    q = qb[pl.ds(q_row, BLOCK), lanes] * jnp.asarray(1.0 / math.sqrt(head_dim), dtype)
    g = gb[pl.ds(q_row, BLOCK), lanes]
    q = jnp.concatenate([jnp.where(left, q, zero), jnp.where(left, zero, q)], axis=0)
    g = jnp.concatenate([jnp.where(left, g, zero), jnp.where(left, zero, g)], axis=0)
    keys = kb[window, lanes]
    values = vb[window, lanes]
    by_row = (((1,), (1,)), ((), ()))
    by_key = (((0,), (0,)), ((), ()))
    plain = (((1,), (0,)), ((), ()))
    dot = functools.partial(lax.dot_general, preferred_element_type=jnp.float32)
    scores = dot(keys, q, by_row)
    top = jnp.max(scores, axis=0, keepdims=True)
    weights = jnp.exp(scores - top)
    grad_probs = dot(values, g, by_row)
    scale = 1.0 / jnp.sum(weights, axis=0, keepdims=True)
    row_dot = jnp.sum(weights * grad_probs, axis=0, keepdims=True) * scale
    probs = weights * scale
    low = probs.astype(dtype)
    grad_scores = (probs * (grad_probs - row_dot)).astype(dtype)
    dv[window, lanes] += dot(low, g, plain)
    dk[window, lanes] += dot(grad_scores, q, plain)
    out = dot(values, low, by_key)
    grad_q = dot(keys, grad_scores, by_key) * (1.0 / math.sqrt(head_dim))

    def diagonal(x):
        return jnp.concatenate([x[:head_dim, :BLOCK], x[head_dim:, BLOCK:]], axis=0).T.astype(dtype)

    ob[pl.ds(q_row, BLOCK), lanes] = diagonal(out)
    dqb[pl.ds(q_row, BLOCK), lanes] = diagonal(grad_q)


def attend_kernel(
    blocks, piece, width, head_dim,
    starts, ends, place, q, k, v, g, inter, intra, inter_head, intra_head, *rest
):
    if piece:
        rest = rest[2:]
    attended, grad_q, back_inter, back_intra, grad_k, grad_v = rest[:6]
    kb, vb, qb, gb, dk, dv, ob, dqb, low, head, sem = rest[6:]
    first, odd = place[0], place[1]
    cols = pl.ds(piece * width, width)
    own = rows(SLOTS, blocks)
    count = [0]

    def copy(source, target):
        count[0] += 1
        return pltpu.make_async_copy(source, target, sem.at[count[0] - 1])

    heads = [
        copy(inter_head.at[pl.ds(2 * SLOTS * BLOCK, HEADER)], head.at[0]),
        copy(intra_head.at[pl.ds(2 * SLOTS * BLOCK, HEADER)], head.at[1]),
    ]
    loads = [
        copy(k.at[:, cols], kb.at[own]),
        copy(v.at[:, cols], vb.at[own]),
        copy(q.at[:, cols], qb.at[rows(1, blocks)]),
        copy(g.at[:, cols], gb.at[rows(1, blocks)]),
    ]
    for c in heads + loads:
        c.start()
    is_odd = odd == 1
    for c in heads:
        c.wait()
    from_inter = jnp.max(head[0].astype(jnp.float32)).astype(jnp.int32)
    from_intra = jnp.max(head[1].astype(jnp.float32)).astype(jnp.int32)
    below_span = jnp.where(is_odd, from_intra, from_inter)
    above_span = jnp.where(is_odd, from_inter, from_intra)

    near_below, far_below = SLOTS - 1, SLOTS - 2
    near_above, far_above = SLOTS + blocks, SLOTS + blocks + 1
    base = count[0]

    def arrive(message, near, far, target, span, slot):
        at = lambda i: sem.at[base + slot * 4 + i]
        part = lambda i: message.at[rows(i)]
        make = pltpu.make_async_copy
        always = [make(part(0), kb.at[rows(near)], at(0)), make(part(1), vb.at[rows(near)], at(1))]
        moved = [make(part(2), qb.at[rows(target)], at(2)), make(part(3), gb.at[rows(target)], at(3))]
        stays = [make(part(2), kb.at[rows(far)], at(2)), make(part(3), vb.at[rows(far)], at(3))]
        for c in always:
            c.start()

        @pl.when(span > 0)
        def _():
            for c in moved:
                c.start()

        @pl.when(span == 0)
        def _():
            for c in stays:
                c.start()

        return always + stays

    inter_near = jnp.where(is_odd, near_above, near_below)
    inter_far = jnp.where(is_odd, far_above, far_below)
    inter_target = jnp.where(is_odd, blocks + 1, 0)
    intra_near = jnp.where(is_odd, near_below, near_above)
    intra_far = jnp.where(is_odd, far_below, far_above)
    intra_target = jnp.where(is_odd, 0, blocks + 1)
    loads += arrive(inter, inter_near, inter_far, inter_target, from_inter, 0)
    loads += arrive(intra, intra_near, intra_far, intra_target, from_intra, 1)
    dk[...] = jnp.zeros_like(dk)
    dv[...] = jnp.zeros_like(dv)
    for c in loads:
        c.wait()

    up = moved_up(starts, ends, first, blocks)
    down = moved_down(starts, ends, first)

    def task(index, carry):
        mine = jnp.clip(index - 1, 0, blocks - 1)
        lower, upper = index == 0, index == blocks + 1
        span = ends[mine] - starts[mine]
        gone = ((index == 1) & down) | ((index == blocks) & up)
        span = jnp.where(gone, 0, span)
        span = jnp.where(lower, below_span, jnp.where(upper, above_span, span))
        window = starts[mine] - first + SLOTS
        window = jnp.where(lower, near_below, jnp.where(upper, near_above - REACH, window))
        q_row = pl.multiple_of(index * BLOCK, BLOCK)
        k_row = pl.multiple_of(window * BLOCK, BLOCK)
        for size in range(1, MAX_BAND + 1):

            @pl.when(span == size)
            def _():
                @pl.loop(0, width // (2 * head_dim))
                def _(pair):
                    lane = pl.multiple_of(pair * 2 * head_dim, 2 * head_dim)
                    attend_pair(size, head_dim, q_row, k_row, lane, kb, vb, qb, gb, dk, dv, ob, dqb)

        return carry

    lax.fori_loop(0, blocks + 2, task, 0)

    stores = [
        (ob.at[rows(1, blocks)], attended.at[:, cols]),
        (dqb.at[rows(1, blocks)], grad_q.at[:, cols]),
        (dk.at[own], grad_k),
        (dv.at[own], grad_v),
    ]
    stores = [pltpu.make_async_copy(a, b, sem.at[i]) for i, (a, b) in enumerate(stores)]
    for c in stores:
        c.start()

    def leave(message, near, far, target, span, slot):
        at = lambda i: sem.at[base + slot * 2 + i]
        low[slot, rows(0)] = dk[rows(near)].astype(low.dtype)
        low[slot, rows(1)] = dv[rows(near)].astype(low.dtype)

        @pl.when(span > 0)
        def _():
            low[slot, rows(2)] = ob[rows(target)]
            low[slot, rows(3)] = dqb[rows(target)]

        @pl.when(span == 0)
        def _():
            low[slot, rows(2)] = dk[rows(far)].astype(low.dtype)
            low[slot, rows(3)] = dv[rows(far)].astype(low.dtype)

        c = pltpu.make_async_copy(low.at[slot], message, at(0))
        c.start()
        return [c]

    stores += leave(back_inter, inter_near, inter_far, inter_target, from_inter, 0)
    stores += leave(back_intra, intra_near, intra_far, intra_target, from_intra, 1)
    for c in stores:
        c.wait()


def attend(blocks, piece, width, head_dim, starts, ends, place, q, k, v, g, inter, intra, heads, outs):
    low, high = q.dtype, jnp.float32
    back = jax.ShapeDtypeStruct((2 * SLOTS * BLOCK, width), low)
    whole = jax.ShapeDtypeStruct(q.shape, low)
    total = jax.ShapeDtypeStruct((blocks * BLOCK, width), high)
    sources, targets = (blocks + 2 * SLOTS) * BLOCK, (blocks + 2) * BLOCK
    pairs = blocks * MAX_BAND * (width // (2 * head_dim))
    return pl.pallas_call(
        functools.partial(attend_kernel, blocks, piece, width, head_dim),
        out_shape=(whole, whole, back, back, total, total),
        in_specs=[SMEM] * 3 + [ANY] * (8 + len(outs)),
        out_specs=(ANY,) * 6,
        input_output_aliases={11: 0, 12: 1} if outs else {},
        scratch_shapes=[
            pltpu.VMEM((sources, width), low),
            pltpu.VMEM((sources, width), low),
            pltpu.VMEM((targets, width), low),
            pltpu.VMEM((targets, width), low),
            pltpu.VMEM((sources, width), high),
            pltpu.VMEM((sources, width), high),
            pltpu.VMEM((targets, width), low),
            pltpu.VMEM((targets, width), low),
            pltpu.VMEM((2, 2 * SLOTS * BLOCK, width), low),
            pltpu.VMEM((2, HEADER, width), low),
            pltpu.SemaphoreType.DMA((14,)),
        ],
        compiler_params=pltpu.CompilerParams(vmem_limit_bytes=VMEM_LIMIT),
        cost_estimate=pl.CostEstimate(
            flops=pairs * 12 * BLOCK * 2 * BLOCK * BLOCK, transcendentals=pairs * 2 * BLOCK * BLOCK,
            bytes_accessed=16 * blocks * BLOCK * width,
        ),
        name=f"attend{piece}",
    )(starts, ends, place, q, k, v, g, inter, intra, *heads, *outs)


def settle_kernel(
    blocks, piece, width, starts, ends, place, grad_k, grad_v, inter, intra, *rest
):
    rest = rest[4:] if piece else rest[2:]
    attended, grad_q, out_k, out_v = rest[:4]
    above, below, stage, sem = rest[4:]
    first, odd = place[0], place[1]
    cols = pl.ds(piece * width, width)
    up = moved_up(starts, ends, first, blocks)
    down = moved_down(starts, ends, first)
    is_odd = odd == 1

    @pl.when(is_odd)
    def _():
        run_copies([
            pltpu.make_async_copy(inter, above, sem.at[0]),
            pltpu.make_async_copy(intra, below, sem.at[1]),
        ])

    @pl.when(jnp.logical_not(is_odd))
    def _():
        run_copies([
            pltpu.make_async_copy(intra, above, sem.at[0]),
            pltpu.make_async_copy(inter, below, sem.at[1]),
        ])

    last = blocks - 1
    high = jnp.float32
    keep_up = jnp.logical_not(up)
    keep_down = jnp.logical_not(down)
    for i, (total, stored) in enumerate(((grad_k, stage.at[0]), (grad_v, stage.at[1]))):
        for block in range(blocks):
            value = total[rows(block)]
            if block == 0:
                value += below[rows(i)].astype(high)
            if block == 1:
                far = below[rows(2 + i)].astype(high)
                value += jnp.where(keep_down, far, jnp.zeros_like(far))
            if block == last:
                value += above[rows(i)].astype(high)
            if block == last - 1:
                far = above[rows(2 + i)].astype(high)
                value += jnp.where(keep_up, far, jnp.zeros_like(far))
            stored[rows(block)] = value.astype(stage.dtype)
    stores = [
        pltpu.make_async_copy(stage.at[0], out_k.at[:, cols], sem.at[0]),
        pltpu.make_async_copy(stage.at[1], out_v.at[:, cols], sem.at[1]),
    ]
    for c in stores:
        c.start()

    @pl.when(up)
    def _():
        run_copies([
            pltpu.make_async_copy(above.at[rows(2)], attended.at[rows(last), cols], sem.at[2]),
            pltpu.make_async_copy(above.at[rows(3)], grad_q.at[rows(last), cols], sem.at[3]),
        ])

    @pl.when(down)
    def _():
        run_copies([
            pltpu.make_async_copy(below.at[rows(2)], attended.at[rows(0), cols], sem.at[2]),
            pltpu.make_async_copy(below.at[rows(3)], grad_q.at[rows(0), cols], sem.at[3]),
        ])

    for c in stores:
        c.wait()


def settle(blocks, piece, width, starts, ends, place, grad_k, grad_v, inter, intra, attended, grad_q, outs):
    low = attended.dtype
    whole = jax.ShapeDtypeStruct(attended.shape, low)
    message = 2 * SLOTS * BLOCK
    vmem = pl.BlockSpec(memory_space=pltpu.VMEM)
    aliases = {7: 0, 8: 1}
    if outs:
        aliases.update({9: 2, 10: 3})
    return pl.pallas_call(
        functools.partial(settle_kernel, blocks, piece, width),
        out_shape=(whole,) * 4,
        in_specs=[SMEM] * 3 + [vmem] * 2 + [ANY] * (4 + len(outs)),
        out_specs=(ANY,) * 4,
        input_output_aliases=aliases,
        scratch_shapes=[
            pltpu.VMEM((message, width), low),
            pltpu.VMEM((message, width), low),
            pltpu.VMEM((2, blocks * BLOCK, width), low),
            pltpu.SemaphoreType.DMA((4,)),
        ],
        compiler_params=pltpu.CompilerParams(vmem_limit_bytes=VMEM_LIMIT),
        name=f"settle{piece}",
    )(starts, ends, place, grad_k, grad_v, inter, intra, attended, grad_q, *outs)


def body(q, k, v, g, starts, ends):
    shard_rows, model_width = q.shape
    blocks = shard_rows // BLOCK
    head_dim = model_width // H
    width = model_width // PIECES
    count = lax.axis_size("seq")
    index = lax.axis_index("seq")
    place = jnp.stack([index * blocks, index % 2]).astype(jnp.int32)
    across = [(i, i + 1) for i in range(1, count - 1, 2)] + [(i + 1, i) for i in range(1, count - 1, 2)]
    inside = [(i, i ^ 1) for i in range(count)]
    swap = lambda inter, intra: (lax.ppermute(inter, "seq", across), lax.ppermute(intra, "seq", inside))

    arrived = []
    for piece in range(PIECES):
        arrived.append(swap(*pack(blocks, piece, width, starts, ends, place, q, k, v, g)))
    heads = arrived[0]
    outs, totals, returned = (), [], []
    for piece in range(PIECES):
        results = attend(
            blocks, piece, width, head_dim, starts, ends, place, q, k, v, g, *arrived[piece], heads, outs
        )
        outs = results[:2]
        returned.append(swap(*results[2:4]))
        totals.append(results[4:])
    attended, grad_q = outs
    outs = ()
    for piece in range(PIECES):
        attended, grad_q, *outs = settle(
            blocks, piece, width, starts, ends, place, *totals[piece], *returned[piece], attended, grad_q, outs
        )
    return (attended, grad_q, *outs)


def solution(mesh):
    spec = P(("groups", "seq"), None)
    flat = P(("groups", "seq"))
    return jax.shard_map(
        body,
        mesh=mesh,
        in_specs=(spec, spec, spec, spec, flat, flat),
        out_specs=(spec, spec, spec, spec),
        check_vma=False,
    )
```

```python
import functools
import math

import jax
import jax.numpy as jnp
from jax import lax
from jax.experimental import pallas as pl
from jax.experimental.pallas import tpu as pltpu
from jax.sharding import PartitionSpec as P

H = 16
BLOCK = 128
MAX_BAND = 4
REACH = MAX_BAND - 1
SLOTS = 2
HEADER = 16
PIECES = (2, 4, 2)
VMEM_LIMIT = 28 * 1024 * 1024
SMALL_LIMIT = 12 * 1024 * 1024
PACK_LIMIT = 56 * 1024 * 1024
SETTLE_WEIGHT = 8

ANY = pl.BlockSpec(memory_space=pl.ANY)
SMEM = pl.BlockSpec(memory_space=pltpu.SMEM)


def rows(block, count=1):
    if isinstance(block, int):
        return pl.ds(block * BLOCK, count * BLOCK)
    return pl.ds(pl.multiple_of(block * BLOCK, BLOCK), count * BLOCK)


def position(blocks):
    index = lax.axis_index("seq")
    return index * blocks, lax.rem(index, 2) == 1


def run_copies(copies):
    for copy in copies:
        copy.start()
    for copy in copies:
        copy.wait()


def moved_up(starts, ends, first, blocks):
    return ends[blocks - 1] == first + blocks + REACH


def moved_down(starts, ends, first):
    return starts[0] == first - REACH


def pack_kernel(blocks, windows, starts, ends, q, k, v, g, *rest):
    count = len(windows)
    messages, stages, sem = rest[-2 * count - 1 : -count - 1], rest[-count - 1 : -1], rest[-1]
    first, is_odd = position(blocks)
    up = moved_up(starts, ends, first, blocks)
    down = moved_down(starts, ends, first)
    make = pltpu.make_async_copy

    def gather(edge, behind, moves, index):
        low, width = windows[index][:2]
        cols = pl.ds(low, width)

        def copy(source, block, part):
            return make(source.at[rows(block), cols], stages[index].at[rows(part)], sem.at[index * 5 + part])

        near = [copy(k, edge, 0), copy(v, edge, 1)]
        target = [copy(q, edge, 2), copy(g, edge, 3)]
        far = [copy(k, behind, 2), copy(v, behind, 3)]
        for c in near:
            c.start()

        @pl.when(moves)
        def _():
            for c in target:
                c.start()

        @pl.when(jnp.logical_not(moves))
        def _():
            for c in far:
                c.start()

        return near + far

    up_value = jnp.where(up, MAX_BAND, 0)
    down_value = jnp.where(down, ends[0] - starts[0], 0)
    waits, values = [], []
    for index, (_, _, _, intra) in enumerate(windows):
        above = jnp.logical_not(is_odd) if intra else is_odd
        moves = (above & up) | (jnp.logical_not(above) & down)
        edge = jnp.where(above, blocks - 1, 0)
        behind = jnp.where(above, blocks - 2, 1)
        waits.append(gather(edge, behind, moves, index))
        values.append(jnp.where(above, up_value, down_value))
    sends = []
    for index, (_, width, header, _) in enumerate(windows):
        if header:
            stages[index][pl.ds(2 * SLOTS * BLOCK, HEADER)] = jnp.full(
                (HEADER, width), values[index].astype(jnp.float32)
            ).astype(stages[index].dtype)
        for c in waits[index]:
            c.wait()
        sends.append(make(stages[index], messages[index], sem.at[index * 5 + 4]))
        sends[-1].start()
    for c in sends:
        c.wait()


def pack(name, blocks, windows, starts, ends, q, k, v, g, *after):
    shapes = tuple(
        jax.ShapeDtypeStruct((2 * SLOTS * BLOCK + (HEADER if header else 0), width), q.dtype)
        for _, width, header, _ in windows
    )
    return pl.pallas_call(
        functools.partial(pack_kernel, blocks, windows),
        out_shape=shapes,
        in_specs=[SMEM] * 2 + [ANY] * (4 + len(after)),
        out_specs=(ANY,) * len(shapes),
        scratch_shapes=[pltpu.VMEM(shape.shape, q.dtype) for shape in shapes]
        + [pltpu.SemaphoreType.DMA((5 * len(shapes),))],
        compiler_params=pltpu.CompilerParams(vmem_limit_bytes=PACK_LIMIT),
        cost_estimate=pl.CostEstimate(
            flops=0, transcendentals=0, bytes_accessed=sum(4 * math.prod(shape.shape) for shape in shapes)
        ),
        name=name,
    )(starts, ends, q, k, v, g, *after)


def attend_pairs(count, head_dim, pairs, q_row, k_row, kb, vb, qb, gb, dk, dv, ob, dqb):
    dtype = kb.dtype
    scale = 1.0 / math.sqrt(head_dim)
    window = pl.ds(k_row, count * BLOCK)
    block = pl.ds(q_row, BLOCK)
    left = lax.broadcasted_iota(jnp.int32, (BLOCK, 2 * head_dim), 1) < head_dim
    zero = jnp.zeros((BLOCK, 2 * head_dim), dtype)
    by_row = (((1,), (1,)), ((), ()))
    by_key = (((0,), (0,)), ((), ()))
    plain = (((1,), (0,)), ((), ()))
    dot = functools.partial(lax.dot_general, preferred_element_type=jnp.float32)

    def split(x):
        return jnp.concatenate([jnp.where(left, x, zero), jnp.where(left, zero, x)], axis=0)

    def diagonal(x):
        return jnp.concatenate([x[:head_dim, :BLOCK], x[head_dim:, BLOCK:]], axis=0).T.astype(dtype)

    fronts = []
    for pair in range(pairs):
        lanes = pl.ds(pair * 2 * head_dim, 2 * head_dim)
        q = split(qb[block, lanes] * jnp.asarray(scale, dtype))
        g = split(gb[block, lanes])
        keys, values = kb[window, lanes], vb[window, lanes]
        fronts.append((lanes, q, g, keys, values, dot(keys, q, by_row), dot(values, g, by_row)))
    middles = []
    for lanes, q, g, keys, values, scores, grad_probs in fronts:
        weights = jnp.exp(scores - jnp.max(scores, axis=0, keepdims=True))
        total = 1.0 / jnp.sum(weights, axis=0, keepdims=True)
        row_dot = jnp.sum(weights * grad_probs, axis=0, keepdims=True) * total
        probs = weights * total
        middles.append((probs.astype(dtype), (probs * (grad_probs - row_dot)).astype(dtype)))
    for (lanes, q, g, keys, values, _, _), (probs, grad_scores) in zip(fronts, middles):
        out = dot(values, probs, by_key)
        grad_q = dot(keys, grad_scores, by_key) * scale
        add_v = dot(probs, g, plain)
        add_k = dot(grad_scores, q, plain)
        ob[block, lanes] = diagonal(out)
        dqb[block, lanes] = diagonal(grad_q)
        dv[window, lanes] += add_v
        dk[window, lanes] += add_k


def attend_kernel(
    blocks, low_col, width, intra_col, head_dim,
    starts, ends, q, k, v, g, inter, intra, inter_head, intra_head, *rest
):
    attended, grad_q, back_intra, back_inter, grad_k, grad_v = rest[-17:-11]
    kb, vb, qb, gb, dk, dv, ob, dqb, low, head, sem = rest[-11:]
    first, is_odd = position(blocks)
    cols = pl.ds(low_col, width)
    own = rows(SLOTS, blocks)
    make = pltpu.make_async_copy
    note = pl.ds(2 * SLOTS * BLOCK, HEADER)
    heads = [
        make(inter_head.at[note, pl.ds(0, BLOCK)], head.at[0], sem.at[0]),
        make(intra_head.at[note, pl.ds(0, BLOCK)], head.at[1], sem.at[1]),
    ]
    loads = [
        make(k.at[:, cols], kb.at[own], sem.at[2]),
        make(v.at[:, cols], vb.at[own], sem.at[3]),
        make(q.at[:, cols], qb.at[rows(1, blocks)], sem.at[4]),
        make(g.at[:, cols], gb.at[rows(1, blocks)], sem.at[5]),
    ]
    for c in heads + loads:
        c.start()
    for c in heads:
        c.wait()
    from_inter = jnp.max(head[0].astype(jnp.float32)).astype(jnp.int32)
    from_intra = jnp.max(head[1].astype(jnp.float32)).astype(jnp.int32)
    below_span = jnp.where(is_odd, from_intra, from_inter)
    above_span = jnp.where(is_odd, from_inter, from_intra)

    near_below, far_below = SLOTS - 1, SLOTS - 2
    near_above, far_above = SLOTS + blocks, SLOTS + blocks + 1
    base = 6

    def arrive(message, near, far, target, span, slot):
        at = lambda i: sem.at[base + slot * 4 + i]
        always = [make(message(0), kb.at[rows(near)], at(0)), make(message(1), vb.at[rows(near)], at(1))]
        moved = [make(message(2), qb.at[rows(target)], at(2)), make(message(3), gb.at[rows(target)], at(3))]
        stays = [make(message(2), kb.at[rows(far)], at(2)), make(message(3), vb.at[rows(far)], at(3))]
        for c in always:
            c.start()

        @pl.when(span > 0)
        def _():
            for c in moved:
                c.start()

        @pl.when(span == 0)
        def _():
            for c in stays:
                c.start()

        return always + stays

    inter_near = jnp.where(is_odd, near_above, near_below)
    inter_far = jnp.where(is_odd, far_above, far_below)
    inter_target = jnp.where(is_odd, blocks + 1, 0)
    intra_near = jnp.where(is_odd, near_below, near_above)
    intra_far = jnp.where(is_odd, far_below, far_above)
    intra_target = jnp.where(is_odd, 0, blocks + 1)
    loads += arrive(lambda i: inter.at[rows(i)], inter_near, inter_far, inter_target, from_inter, 0)
    columns = pl.ds(intra_col, width)
    loads += arrive(lambda i: intra.at[rows(i), columns], intra_near, intra_far, intra_target, from_intra, 1)
    dk[...] = jnp.zeros_like(dk)
    dv[...] = jnp.zeros_like(dv)
    for c in loads:
        c.wait()

    up = moved_up(starts, ends, first, blocks)
    down = moved_down(starts, ends, first)

    def task(index, carry):
        mine = jnp.clip(index - 1, 0, blocks - 1)
        lower, upper = index == 0, index == blocks + 1
        span = ends[mine] - starts[mine]
        gone = ((index == 1) & down) | ((index == blocks) & up)
        span = jnp.where(gone, 0, span)
        span = jnp.where(lower, below_span, jnp.where(upper, above_span, span))
        window = starts[mine] - first + SLOTS
        window = jnp.where(lower, near_below, jnp.where(upper, near_above - REACH, window))
        q_row = pl.multiple_of(index * BLOCK, BLOCK)
        k_row = pl.multiple_of(window * BLOCK, BLOCK)
        for size in range(1, MAX_BAND + 1):

            @pl.when(span == size)
            def _():
                attend_pairs(
                    size, head_dim, width // (2 * head_dim), q_row, k_row, kb, vb, qb, gb, dk, dv, ob, dqb
                )

        return carry

    lax.fori_loop(0, blocks + 2, task, 0)

    def leave(target, near, far, block, span, slot):
        low[slot, rows(0)] = dk[rows(near)].astype(low.dtype)
        low[slot, rows(1)] = dv[rows(near)].astype(low.dtype)

        @pl.when(span > 0)
        def _():
            low[slot, rows(2)] = ob[rows(block)]
            low[slot, rows(3)] = dqb[rows(block)]

        @pl.when(span == 0)
        def _():
            low[slot, rows(2)] = dk[rows(far)].astype(low.dtype)
            low[slot, rows(3)] = dv[rows(far)].astype(low.dtype)

        c = make(low.at[slot], target, sem.at[slot])
        c.start()
        return c

    stores = [leave(back_inter, inter_near, inter_far, inter_target, from_inter, 0)]
    stores += [
        make(ob.at[rows(1, blocks)], attended.at[:, cols], sem.at[2]),
        make(dqb.at[rows(1, blocks)], grad_q.at[:, cols], sem.at[3]),
        make(dk.at[own], grad_k, sem.at[4]),
        make(dv.at[own], grad_v, sem.at[5]),
    ]
    for c in stores[1:]:
        c.start()
    stores.append(leave(back_intra, intra_near, intra_far, intra_target, from_intra, 1))
    for c in stores:
        c.wait()


def attend(name, blocks, low_col, width, intra_col, head_dim, starts, ends, q, k, v, g, messages, outs, after):
    low, high = q.dtype, jnp.float32
    message = 2 * SLOTS * BLOCK
    whole = jax.ShapeDtypeStruct(q.shape, low)
    back = jax.ShapeDtypeStruct((message, width), low)
    total = jax.ShapeDtypeStruct((blocks * BLOCK, width), high)
    sources, targets = (blocks + 2 * SLOTS) * BLOCK, (blocks + 2) * BLOCK
    pairs = blocks * MAX_BAND * (width // (2 * head_dim))
    return pl.pallas_call(
        functools.partial(attend_kernel, blocks, low_col, width, intra_col, head_dim),
        out_shape=(whole, whole, back, back, total, total),
        in_specs=[SMEM] * 2 + [ANY] * (8 + len(outs) + len(after)),
        out_specs=(ANY,) * 6,
        input_output_aliases={10 + i: i for i in range(len(outs))},
        scratch_shapes=[
            pltpu.VMEM((sources, width), low),
            pltpu.VMEM((sources, width), low),
            pltpu.VMEM((targets, width), low),
            pltpu.VMEM((targets, width), low),
            pltpu.VMEM((sources, width), high),
            pltpu.VMEM((sources, width), high),
            pltpu.VMEM((targets, width), low),
            pltpu.VMEM((targets, width), low),
            pltpu.VMEM((2, message, width), low),
            pltpu.VMEM((2, HEADER, BLOCK), low),
            pltpu.SemaphoreType.DMA((14,)),
        ],
        compiler_params=pltpu.CompilerParams(vmem_limit_bytes=VMEM_LIMIT),
        cost_estimate=pl.CostEstimate(
            flops=4 * pairs * 12 * BLOCK * 2 * BLOCK * BLOCK, transcendentals=pairs * 2 * BLOCK * BLOCK,
            bytes_accessed=16 * blocks * BLOCK * width,
        ),
        name=name,
    )(starts, ends, q, k, v, g, *messages, *outs, *after)


def settle_kernel(blocks, parts, starts, ends, *refs):
    count = len(parts)
    totals, messages = refs[: 2 * count], refs[2 * count : 3 * count]
    attended, grad_q, out_k, out_v = refs[-3 * count - 5 : -3 * count - 1]
    landed, sums = refs[-3 * count - 1 : -2 * count - 1], refs[-2 * count - 1 : -count - 1]
    stages, sem = refs[-count - 1 : -1], refs[-1]
    first, is_odd = position(blocks)
    up = moved_up(starts, ends, first, blocks)
    down = moved_down(starts, ends, first)
    make = pltpu.make_async_copy
    sides = []
    for _, _, intra in parts:
        above = jnp.logical_not(is_odd) if intra else is_odd
        near = jnp.where(above, blocks - 1, 0)
        far = jnp.where(above, blocks - 2, 1)
        sides.append((near, far, (above & up) | (jnp.logical_not(above) & down)))
    loads = []
    for i in range(count):
        near, far, _ = sides[i]
        loads.append([
            make(messages[i], landed[i], sem.at[i, 0]),
            make(totals[2 * i].at[rows(near)], sums[i].at[rows(0)], sem.at[i, 1]),
            make(totals[2 * i + 1].at[rows(near)], sums[i].at[rows(1)], sem.at[i, 2]),
            make(totals[2 * i].at[rows(far)], sums[i].at[rows(2)], sem.at[i, 3]),
            make(totals[2 * i + 1].at[rows(far)], sums[i].at[rows(3)], sem.at[i, 4]),
        ])
        for c in loads[-1]:
            c.start()
    stores = []
    for i, (low_col, width, _) in enumerate(parts):
        cols = pl.ds(low_col, width)
        near, far, moved = sides[i]
        keep = jnp.logical_not(moved)
        for c in loads[i]:
            c.wait()
        for half in range(2):
            came = landed[i][rows(2 * half, 2)].astype(jnp.float32)
            if half:
                came = jnp.where(keep, came, jnp.zeros_like(came))
            stages[i][rows(2 * half, 2)] = (sums[i][rows(2 * half, 2)] + came).astype(stages[i].dtype)
            block = far if half else near
            stores += [
                make(stages[i].at[rows(2 * half)], out_k.at[rows(block), cols], sem.at[i, 2 * half]),
                make(stages[i].at[rows(2 * half + 1)], out_v.at[rows(block), cols], sem.at[i, 2 * half + 1]),
            ]
            for c in stores[-2:]:
                c.start()

        @pl.when(moved)
        def _():
            run_copies([
                make(landed[i].at[rows(2)], attended.at[rows(near), cols], sem.at[i, 4]),
                make(landed[i].at[rows(3)], grad_q.at[rows(near), cols], sem.at[i, 5]),
            ])

    for c in stores:
        c.wait()


def settle(name, blocks, parts, starts, ends, totals, messages, outs):
    low = outs[0].dtype
    whole = jax.ShapeDtypeStruct(outs[0].shape, low)
    count = len(parts)
    shapes = [(2 * SLOTS * BLOCK, width) for _, width, _ in parts]
    base = 2 + 3 * count
    return pl.pallas_call(
        functools.partial(settle_kernel, blocks, parts),
        out_shape=(whole,) * 4,
        in_specs=[SMEM] * 2 + [ANY] * (3 * count + len(outs)),
        out_specs=(ANY,) * 4,
        input_output_aliases={base + i: i for i in range(len(outs))},
        scratch_shapes=[pltpu.VMEM(shape, low) for shape in shapes]
        + [pltpu.VMEM(shape, jnp.float32) for shape in shapes]
        + [pltpu.VMEM(shape, low) for shape in shapes]
        + [pltpu.SemaphoreType.DMA((count, 6))],
        compiler_params=pltpu.CompilerParams(vmem_limit_bytes=SMALL_LIMIT),
        cost_estimate=pl.CostEstimate(
            flops=0, transcendentals=0, bytes_accessed=sum(SETTLE_WEIGHT * math.prod(shape) for shape in shapes)
        ),
        name=name,
    )(starts, ends, *totals, *messages, *outs)


def body(q, k, v, g, starts, ends):
    shard_rows, model_width = q.shape
    blocks = shard_rows // BLOCK
    head_dim = model_width // H
    count = lax.axis_size("seq")
    across = [(i, i + 1) for i in range(1, count - 1, 2)] + [(i + 1, i) for i in range(1, count - 1, 2)]
    inside = [(i, i ^ 1) for i in range(count)]
    pieces, low_col = [], 0
    for pairs in PIECES:
        pieces.append((low_col, pairs * 2 * head_dim))
        low_col += pairs * 2 * head_dim

    first, rest = pieces[0], pieces[1:]
    last = len(pieces) - 1
    swap = lambda x, pairs: lax.ppermute(x, "seq", pairs)
    rest_col = first[1]

    def send(i, after):
        windows = [(*pieces[i], i == 0, False)]
        if i == 0:
            windows.append((*first, True, True))
        elif i == 1:
            windows.append((rest_col, model_width - rest_col, False, True))
        sent = pack(f"pack{i}", blocks, windows, starts, ends, q, k, v, g, *after)
        return sent[0], swap(sent[0], across), swap(sent[1], inside) if i < 2 else None

    head, *heads = send(0, ())
    _, inter, intra_rest = send(1, (head,))
    arrived = [heads, (inter, intra_rest)]

    outs, totals, returned = (), [], []
    for i, piece in enumerate(pieces):
        results = attend(
            f"attend{i}", blocks, *piece, piece[0] - rest_col if i else 0, head_dim, starts, ends, q, k, v, g,
            (*arrived[i], *heads), outs, returned[i - 2] if i > 1 else (),
        )
        outs = results[:2]
        if i + 2 <= last:
            arrived.append((send(i + 2, (results[3],))[1], intra_rest))
        returned.append((swap(results[3], across), swap(results[2], inside)))
        totals.append(results[4:])
    for name, members in (("settle_a", range(last)), ("settle_b", (last,))):
        parts = [(*pieces[i], inner) for i in members for inner in (False, True)]
        outs = settle(
            name, blocks, parts, starts, ends, [x for i in members for _ in range(2) for x in totals[i]],
            [x for i in members for x in returned[i]], outs,
        )
    return outs


def solution(mesh):
    spec = P(("groups", "seq"), None)
    flat = P(("groups", "seq"))
    return jax.shard_map(
        body,
        mesh=mesh,
        in_specs=(spec, spec, spec, spec, flat, flat),
        out_specs=(spec, spec, spec, spec),
        check_vma=False,
    )
```

```python
import functools
import math

import jax
import jax.numpy as jnp
from jax import lax
from jax.experimental import pallas as pl
from jax.experimental.pallas import tpu as pltpu
from jax.sharding import PartitionSpec as P

H = 16
BLOCK = 128
MAX_BAND = 4
REACH = MAX_BAND - 1
SLOTS = 2
HEADER = 16
PIECES = (2, 4, 2)
VMEM_LIMIT = 28 * 1024 * 1024
SMALL_LIMIT = 12 * 1024 * 1024
PACK_LIMIT = 56 * 1024 * 1024
SETTLE_WEIGHT = 8

ANY = pl.BlockSpec(memory_space=pl.ANY)
SMEM = pl.BlockSpec(memory_space=pltpu.SMEM)


def rows(block, count=1):
    if isinstance(block, int):
        return pl.ds(block * BLOCK, count * BLOCK)
    return pl.ds(pl.multiple_of(block * BLOCK, BLOCK), count * BLOCK)


def position(blocks):
    index = lax.axis_index("seq")
    return index * blocks, lax.rem(index, 2) == 1


def run_copies(copies):
    for copy in copies:
        copy.start()
    for copy in copies:
        copy.wait()


def moved_up(starts, ends, first, blocks):
    return ends[blocks - 1] == first + blocks + REACH


def moved_down(starts, ends, first):
    return starts[0] == first - REACH


def edge(blocks, above, up, down):
    near = jnp.where(above, blocks - 1, 0)
    far = jnp.where(above, blocks - 2, 1)
    return near, far, (above & up) | (jnp.logical_not(above) & down)


def gather(side, cols, q, k, v, g, target, sem):
    near, far, moved = side

    def copy(source, block, part):
        return pltpu.make_async_copy(source.at[rows(block), cols], target.at[rows(part)], sem(part))

    always = [copy(k, near, 0), copy(v, near, 1)]
    goes = [copy(q, near, 2), copy(g, near, 3)]
    stays = [copy(k, far, 2), copy(v, far, 3)]
    for c in always:
        c.start()

    @pl.when(moved)
    def _():
        for c in goes:
            c.start()

    @pl.when(jnp.logical_not(moved))
    def _():
        for c in stays:
            c.start()

    return always + stays


def pack_kernel(blocks, windows, starts, ends, q, k, v, g, *rest):
    count = len(windows)
    messages, stages, sem = rest[-2 * count - 1 : -count - 1], rest[-count - 1 : -1], rest[-1]
    first, is_odd = position(blocks)
    up = moved_up(starts, ends, first, blocks)
    down = moved_down(starts, ends, first)
    up_value = jnp.where(up, MAX_BAND, 0)
    down_value = jnp.where(down, ends[0] - starts[0], 0)
    waits, values = [], []
    for index, (low, width, _, intra) in enumerate(windows):
        above = jnp.logical_not(is_odd) if intra else is_odd
        side = edge(blocks, above, up, down)
        at = lambda part, index=index: sem.at[index * 5 + part]
        waits.append(gather(side, pl.ds(low, width), q, k, v, g, stages[index], at))
        values.append(jnp.where(above, up_value, down_value))
    sends = []
    for index, (_, width, header, _) in enumerate(windows):
        if header:
            stages[index][pl.ds(2 * SLOTS * BLOCK, HEADER)] = jnp.full(
                (HEADER, width), values[index].astype(jnp.float32)
            ).astype(stages[index].dtype)
        for c in waits[index]:
            c.wait()
        sends.append(pltpu.make_async_copy(stages[index], messages[index], sem.at[index * 5 + 4]))
        sends[-1].start()
    for c in sends:
        c.wait()


def pack(name, blocks, windows, starts, ends, q, k, v, g, *after):
    shapes = tuple(
        jax.ShapeDtypeStruct((2 * SLOTS * BLOCK + (HEADER if header else 0), width), q.dtype)
        for _, width, header, _ in windows
    )
    return pl.pallas_call(
        functools.partial(pack_kernel, blocks, windows),
        out_shape=shapes,
        in_specs=[SMEM] * 2 + [ANY] * (4 + len(after)),
        out_specs=(ANY,) * len(shapes),
        scratch_shapes=[pltpu.VMEM(shape.shape, q.dtype) for shape in shapes]
        + [pltpu.SemaphoreType.DMA((5 * len(shapes),))],
        compiler_params=pltpu.CompilerParams(vmem_limit_bytes=PACK_LIMIT),
        cost_estimate=pl.CostEstimate(
            flops=0, transcendentals=0, bytes_accessed=sum(4 * math.prod(shape.shape) for shape in shapes)
        ),
        name=name,
    )(starts, ends, q, k, v, g, *after)


def attend_pairs(count, head_dim, pairs, q_row, k_row, kb, vb, qb, gb, dk, dv, ob, dqb):
    dtype = kb.dtype
    scale = 1.0 / math.sqrt(head_dim)
    window = pl.ds(k_row, count * BLOCK)
    block = pl.ds(q_row, BLOCK)
    left = lax.broadcasted_iota(jnp.int32, (BLOCK, 2 * head_dim), 1) < head_dim
    zero = jnp.zeros((BLOCK, 2 * head_dim), dtype)
    by_row = (((1,), (1,)), ((), ()))
    by_key = (((0,), (0,)), ((), ()))
    plain = (((1,), (0,)), ((), ()))
    dot = functools.partial(lax.dot_general, preferred_element_type=jnp.float32)

    def split(x):
        return jnp.concatenate([jnp.where(left, x, zero), jnp.where(left, zero, x)], axis=0)

    def diagonal(x):
        return jnp.concatenate([x[:head_dim, :BLOCK], x[head_dim:, BLOCK:]], axis=0).T.astype(dtype)

    fronts = []
    for pair in range(pairs):
        lanes = pl.ds(pair * 2 * head_dim, 2 * head_dim)
        q = split(qb[block, lanes] * jnp.asarray(scale, dtype))
        g = split(gb[block, lanes])
        keys, values = kb[window, lanes], vb[window, lanes]
        fronts.append((lanes, q, g, keys, values, dot(keys, q, by_row), dot(values, g, by_row)))
    middles = []
    for lanes, q, g, keys, values, scores, grad_probs in fronts:
        weights = jnp.exp(scores - jnp.max(scores, axis=0, keepdims=True))
        total = 1.0 / jnp.sum(weights, axis=0, keepdims=True)
        row_dot = jnp.sum(weights * grad_probs, axis=0, keepdims=True) * total
        probs = weights * total
        middles.append((probs.astype(dtype), (probs * (grad_probs - row_dot)).astype(dtype)))
    for (lanes, q, g, keys, values, _, _), (probs, grad_scores) in zip(fronts, middles):
        out = dot(values, probs, by_key)
        grad_q = dot(keys, grad_scores, by_key) * scale
        add_v = dot(probs, g, plain)
        add_k = dot(grad_scores, q, plain)
        ob[block, lanes] = diagonal(out)
        dqb[block, lanes] = diagonal(grad_q)
        dv[window, lanes] += add_v
        dk[window, lanes] += add_k


def attend_kernel(
    blocks, low_col, width, inter_row, intra_col, forward_col, head_dim,
    starts, ends, q, k, v, g, inter, intra, inter_head, intra_head, *rest
):
    attended, grad_q, back_intra, back_inter, grad_k, grad_v = rest[-18:-12]
    kb, vb, qb, gb, dk, dv, ob, dqb, low, head, ahead, sem = rest[-12:]
    first, is_odd = position(blocks)
    cols = pl.ds(low_col, width)
    own = rows(SLOTS, blocks)
    make = pltpu.make_async_copy
    note = pl.ds(2 * SLOTS * BLOCK, HEADER)
    heads = [
        make(inter_head.at[note, pl.ds(0, BLOCK)], head.at[0], sem.at[0]),
        make(intra_head.at[note, pl.ds(0, BLOCK)], head.at[1], sem.at[1]),
    ]
    loads = [
        make(k.at[:, cols], kb.at[own], sem.at[2]),
        make(v.at[:, cols], vb.at[own], sem.at[3]),
        make(q.at[:, cols], qb.at[rows(1, blocks)], sem.at[4]),
        make(g.at[:, cols], gb.at[rows(1, blocks)], sem.at[5]),
    ]
    for c in heads + loads:
        c.start()
    for c in heads:
        c.wait()
    up = moved_up(starts, ends, first, blocks)
    down = moved_down(starts, ends, first)
    onward = []
    if forward_col is not None:
        onward = gather(
            edge(blocks, is_odd, up, down), pl.ds(forward_col, width), q, k, v, g, ahead, lambda i: sem.at[14 + i]
        )
    from_inter = jnp.max(head[0].astype(jnp.float32)).astype(jnp.int32)
    from_intra = jnp.max(head[1].astype(jnp.float32)).astype(jnp.int32)
    below_span = jnp.where(is_odd, from_intra, from_inter)
    above_span = jnp.where(is_odd, from_inter, from_intra)

    near_below, far_below = SLOTS - 1, SLOTS - 2
    near_above, far_above = SLOTS + blocks, SLOTS + blocks + 1
    base = 6

    def arrive(message, near, far, target, span, slot):
        at = lambda i: sem.at[base + slot * 4 + i]
        always = [make(message(0), kb.at[rows(near)], at(0)), make(message(1), vb.at[rows(near)], at(1))]
        moved = [make(message(2), qb.at[rows(target)], at(2)), make(message(3), gb.at[rows(target)], at(3))]
        stays = [make(message(2), kb.at[rows(far)], at(2)), make(message(3), vb.at[rows(far)], at(3))]
        for c in always:
            c.start()

        @pl.when(span > 0)
        def _():
            for c in moved:
                c.start()

        @pl.when(span == 0)
        def _():
            for c in stays:
                c.start()

        return always + stays

    inter_near = jnp.where(is_odd, near_above, near_below)
    inter_far = jnp.where(is_odd, far_above, far_below)
    inter_target = jnp.where(is_odd, blocks + 1, 0)
    intra_near = jnp.where(is_odd, near_below, near_above)
    intra_far = jnp.where(is_odd, far_below, far_above)
    intra_target = jnp.where(is_odd, 0, blocks + 1)
    loads += arrive(lambda i: inter.at[pl.ds(inter_row + i * BLOCK, BLOCK)], inter_near, inter_far, inter_target, from_inter, 0)
    columns = pl.ds(intra_col, width)
    loads += arrive(lambda i: intra.at[rows(i), columns], intra_near, intra_far, intra_target, from_intra, 1)
    dk[...] = jnp.zeros_like(dk)
    dv[...] = jnp.zeros_like(dv)
    for c in loads:
        c.wait()
    back = pl.ds(0, 2 * SLOTS * BLOCK)
    for c in onward:
        c.wait()
    if onward:
        onward = [make(ahead, back_inter.at[pl.ds(2 * SLOTS * BLOCK, 2 * SLOTS * BLOCK)], sem.at[14])]
        onward[0].start()

    def task(index, carry):
        mine = jnp.clip(index - 1, 0, blocks - 1)
        lower, upper = index == 0, index == blocks + 1
        span = ends[mine] - starts[mine]
        gone = ((index == 1) & down) | ((index == blocks) & up)
        span = jnp.where(gone, 0, span)
        span = jnp.where(lower, below_span, jnp.where(upper, above_span, span))
        window = starts[mine] - first + SLOTS
        window = jnp.where(lower, near_below, jnp.where(upper, near_above - REACH, window))
        q_row = pl.multiple_of(index * BLOCK, BLOCK)
        k_row = pl.multiple_of(window * BLOCK, BLOCK)
        for size in range(1, MAX_BAND + 1):

            @pl.when(span == size)
            def _():
                attend_pairs(
                    size, head_dim, width // (2 * head_dim), q_row, k_row, kb, vb, qb, gb, dk, dv, ob, dqb
                )

        return carry

    lax.fori_loop(0, blocks + 2, task, 0)

    def leave(target, near, far, block, span, slot):
        low[slot, rows(0)] = dk[rows(near)].astype(low.dtype)
        low[slot, rows(1)] = dv[rows(near)].astype(low.dtype)

        @pl.when(span > 0)
        def _():
            low[slot, rows(2)] = ob[rows(block)]
            low[slot, rows(3)] = dqb[rows(block)]

        @pl.when(span == 0)
        def _():
            low[slot, rows(2)] = dk[rows(far)].astype(low.dtype)
            low[slot, rows(3)] = dv[rows(far)].astype(low.dtype)

        c = make(low.at[slot], target, sem.at[slot])
        c.start()
        return c

    stores = onward + [leave(back_inter.at[back], inter_near, inter_far, inter_target, from_inter, 0)]
    stores += [
        make(ob.at[rows(1, blocks)], attended.at[:, cols], sem.at[2]),
        make(dqb.at[rows(1, blocks)], grad_q.at[:, cols], sem.at[3]),
        make(dk.at[own], grad_k, sem.at[4]),
        make(dv.at[own], grad_v, sem.at[5]),
    ]
    for c in stores[-4:]:
        c.start()
    stores.append(leave(back_intra, intra_near, intra_far, intra_target, from_intra, 1))
    for c in stores:
        c.wait()


def attend(name, blocks, low_col, width, offsets, head_dim, starts, ends, q, k, v, g, messages, outs):
    inter_row, intra_col, forward_col = offsets
    low, high = q.dtype, jnp.float32
    message = 2 * SLOTS * BLOCK
    whole = jax.ShapeDtypeStruct(q.shape, low)
    back = jax.ShapeDtypeStruct((message, width), low)
    joint = back if forward_col is None else jax.ShapeDtypeStruct((2 * message, width), low)
    total = jax.ShapeDtypeStruct((blocks * BLOCK, width), high)
    sources, targets = (blocks + 2 * SLOTS) * BLOCK, (blocks + 2) * BLOCK
    pairs = blocks * MAX_BAND * (width // (2 * head_dim))
    return pl.pallas_call(
        functools.partial(attend_kernel, blocks, low_col, width, inter_row, intra_col, forward_col, head_dim),
        out_shape=(whole, whole, back, joint, total, total),
        in_specs=[SMEM] * 2 + [ANY] * (8 + len(outs)),
        out_specs=(ANY,) * 6,
        input_output_aliases={10 + i: i for i in range(len(outs))},
        scratch_shapes=[
            pltpu.VMEM((sources, width), low),
            pltpu.VMEM((sources, width), low),
            pltpu.VMEM((targets, width), low),
            pltpu.VMEM((targets, width), low),
            pltpu.VMEM((sources, width), high),
            pltpu.VMEM((sources, width), high),
            pltpu.VMEM((targets, width), low),
            pltpu.VMEM((targets, width), low),
            pltpu.VMEM((2, message, width), low),
            pltpu.VMEM((2, HEADER, BLOCK), low),
            pltpu.VMEM((message, width), low),
            pltpu.SemaphoreType.DMA((18,)),
        ],
        compiler_params=pltpu.CompilerParams(vmem_limit_bytes=VMEM_LIMIT),
        cost_estimate=pl.CostEstimate(
            flops=4 * pairs * 12 * BLOCK * 2 * BLOCK * BLOCK, transcendentals=pairs * 2 * BLOCK * BLOCK,
            bytes_accessed=16 * blocks * BLOCK * width,
        ),
        name=name,
    )(starts, ends, q, k, v, g, *messages, *outs)


def settle_kernel(blocks, parts, starts, ends, *refs):
    count = len(parts)
    totals, messages = refs[: 2 * count], refs[2 * count : 3 * count]
    attended, grad_q, out_k, out_v = refs[-3 * count - 5 : -3 * count - 1]
    landed, sums = refs[-3 * count - 1 : -2 * count - 1], refs[-2 * count - 1 : -count - 1]
    stages, sem = refs[-count - 1 : -1], refs[-1]
    first, is_odd = position(blocks)
    up = moved_up(starts, ends, first, blocks)
    down = moved_down(starts, ends, first)
    make = pltpu.make_async_copy
    sides = [edge(blocks, jnp.logical_not(is_odd) if intra else is_odd, up, down) for _, _, intra in parts]
    loads = []
    for i in range(count):
        near, far, _ = sides[i]
        loads.append([
            make(messages[i].at[pl.ds(0, 2 * SLOTS * BLOCK)], landed[i], sem.at[i, 0]),
            make(totals[2 * i].at[rows(near)], sums[i].at[rows(0)], sem.at[i, 1]),
            make(totals[2 * i + 1].at[rows(near)], sums[i].at[rows(1)], sem.at[i, 2]),
            make(totals[2 * i].at[rows(far)], sums[i].at[rows(2)], sem.at[i, 3]),
            make(totals[2 * i + 1].at[rows(far)], sums[i].at[rows(3)], sem.at[i, 4]),
        ])
        for c in loads[-1]:
            c.start()
    stores = []
    for i, (low_col, width, _) in enumerate(parts):
        cols = pl.ds(low_col, width)
        near, far, moved = sides[i]
        keep = jnp.logical_not(moved)
        for c in loads[i]:
            c.wait()
        for half in range(2):
            came = landed[i][rows(2 * half, 2)].astype(jnp.float32)
            if half:
                came = jnp.where(keep, came, jnp.zeros_like(came))
            stages[i][rows(2 * half, 2)] = (sums[i][rows(2 * half, 2)] + came).astype(stages[i].dtype)
            block = far if half else near
            stores += [
                make(stages[i].at[rows(2 * half)], out_k.at[rows(block), cols], sem.at[i, 2 * half]),
                make(stages[i].at[rows(2 * half + 1)], out_v.at[rows(block), cols], sem.at[i, 2 * half + 1]),
            ]
            for c in stores[-2:]:
                c.start()

        @pl.when(moved)
        def _():
            run_copies([
                make(landed[i].at[rows(2)], attended.at[rows(near), cols], sem.at[i, 4]),
                make(landed[i].at[rows(3)], grad_q.at[rows(near), cols], sem.at[i, 5]),
            ])

    for c in stores:
        c.wait()


def settle(name, blocks, parts, starts, ends, totals, messages, outs):
    low = outs[0].dtype
    whole = jax.ShapeDtypeStruct(outs[0].shape, low)
    count = len(parts)
    shapes = [(2 * SLOTS * BLOCK, width) for _, width, _ in parts]
    base = 2 + 3 * count
    return pl.pallas_call(
        functools.partial(settle_kernel, blocks, parts),
        out_shape=(whole,) * 4,
        in_specs=[SMEM] * 2 + [ANY] * (3 * count + len(outs)),
        out_specs=(ANY,) * 4,
        input_output_aliases={base + i: i for i in range(len(outs))},
        scratch_shapes=[pltpu.VMEM(shape, low) for shape in shapes]
        + [pltpu.VMEM(shape, jnp.float32) for shape in shapes]
        + [pltpu.VMEM(shape, low) for shape in shapes]
        + [pltpu.SemaphoreType.DMA((count, 6))],
        compiler_params=pltpu.CompilerParams(vmem_limit_bytes=SMALL_LIMIT),
        cost_estimate=pl.CostEstimate(
            flops=0, transcendentals=0, bytes_accessed=sum(SETTLE_WEIGHT * math.prod(shape) for shape in shapes)
        ),
        name=name,
    )(starts, ends, *totals, *messages, *outs)


def body(q, k, v, g, starts, ends):
    shard_rows, model_width = q.shape
    blocks = shard_rows // BLOCK
    head_dim = model_width // H
    count = lax.axis_size("seq")
    across = [(i, i + 1) for i in range(1, count - 1, 2)] + [(i + 1, i) for i in range(1, count - 1, 2)]
    inside = [(i, i ^ 1) for i in range(count)]
    pieces, low_col = [], 0
    for pairs in PIECES:
        pieces.append((low_col, pairs * 2 * head_dim))
        low_col += pairs * 2 * head_dim

    first, last = pieces[0], len(pieces) - 1
    rest_col = first[1]
    swap = lambda x, pairs: lax.ppermute(x, "seq", pairs)
    inter, intra = pack("pack0", blocks, [(*first, True, False), (*first, True, True)], starts, ends, q, k, v, g)
    heads = (swap(inter, across), swap(intra, inside))
    inter, intra = pack(
        "pack1", blocks, [(*pieces[1], False, False), (rest_col, model_width - rest_col, False, True)],
        starts, ends, q, k, v, g, inter,
    )
    arrived = [heads, (swap(inter, across), swap(intra, inside))]

    outs, totals, returned = (), [], []
    for i, piece in enumerate(pieces):
        if i > 1:
            arrived.append((returned[i - 2][0], arrived[1][1]))
        inter_row = 2 * SLOTS * BLOCK if i > 1 else 0
        intra_col = piece[0] - rest_col if i else 0
        forward_col = pieces[i + 2][0] if i + 2 <= last else None
        results = attend(
            f"attend{i}", blocks, *piece, (inter_row, intra_col, forward_col), head_dim, starts, ends, q, k, v, g,
            (*arrived[i], *heads), outs,
        )
        outs = results[:2]
        returned.append((swap(results[3], across), swap(results[2], inside)))
        totals.append(results[4:])
    for name, members in (("settle_a", range(last)), ("settle_b", (last,))):
        parts = [(*pieces[i], inner) for i in members for inner in (False, True)]
        outs = settle(
            name, blocks, parts, starts, ends, [x for i in members for _ in range(2) for x in totals[i]],
            [x for i in members for x in returned[i]], outs,
        )
    return outs


def solution(mesh):
    spec = P(("groups", "seq"), None)
    flat = P(("groups", "seq"))
    return jax.shard_map(
        body,
        mesh=mesh,
        in_specs=(spec, spec, spec, spec, flat, flat),
        out_specs=(spec, spec, spec, spec),
        check_vma=False,
    )
```

```python
import functools
import math

import jax
import jax.numpy as jnp
from jax import lax
from jax.experimental import pallas as pl
from jax.experimental.pallas import tpu as pltpu
from jax.sharding import PartitionSpec as P

H = 16
BLOCK = 128
MAX_BAND = 4
REACH = MAX_BAND - 1
SLOTS = 2
HEADER = 16
PIECES = (2, 4, 2)
VMEM_LIMIT = 28 * 1024 * 1024
SMALL_LIMIT = 12 * 1024 * 1024
PACK_LIMIT = 56 * 1024 * 1024
SETTLE_WEIGHT = 8

ANY = pl.BlockSpec(memory_space=pl.ANY)
SMEM = pl.BlockSpec(memory_space=pltpu.SMEM)


def rows(block, count=1):
    if isinstance(block, int):
        return pl.ds(block * BLOCK, count * BLOCK)
    return pl.ds(pl.multiple_of(block * BLOCK, BLOCK), count * BLOCK)


def position(blocks):
    index = lax.axis_index("seq")
    return index * blocks, lax.rem(index, 2) == 1


def run_copies(copies):
    for copy in copies:
        copy.start()
    for copy in copies:
        copy.wait()


def moved_up(starts, ends, first, blocks):
    return ends[blocks - 1] == first + blocks + REACH


def moved_down(starts, ends, first):
    return starts[0] == first - REACH


def edge(blocks, above, up, down):
    near = jnp.where(above, blocks - 1, 0)
    far = jnp.where(above, blocks - 2, 1)
    return near, far, (above & up) | (jnp.logical_not(above) & down)


def gather(side, cols, q, k, v, g, target, sem):
    near, far, moved = side

    def copy(source, block, part):
        return pltpu.make_async_copy(source.at[rows(block), cols], target.at[rows(part)], sem(part))

    always = [copy(k, near, 0), copy(v, near, 1)]
    goes = [copy(q, near, 2), copy(g, near, 3)]
    stays = [copy(k, far, 2), copy(v, far, 3)]
    for c in always:
        c.start()

    @pl.when(moved)
    def _():
        for c in goes:
            c.start()

    @pl.when(jnp.logical_not(moved))
    def _():
        for c in stays:
            c.start()

    return always + stays


def pack_kernel(blocks, windows, starts, ends, q, k, v, g, *rest):
    count = len(windows)
    messages, stages, sem = rest[-2 * count - 1 : -count - 1], rest[-count - 1 : -1], rest[-1]
    first, is_odd = position(blocks)
    up = moved_up(starts, ends, first, blocks)
    down = moved_down(starts, ends, first)
    up_value = jnp.where(up, MAX_BAND, 0)
    down_value = jnp.where(down, ends[0] - starts[0], 0)
    waits, values = [], []
    for index, (low, width, _, intra) in enumerate(windows):
        above = jnp.logical_not(is_odd) if intra else is_odd
        side = edge(blocks, above, up, down)
        at = lambda part, index=index: sem.at[index * 5 + part]
        waits.append(gather(side, pl.ds(low, width), q, k, v, g, stages[index], at))
        values.append(jnp.where(above, up_value, down_value))
    sends = []
    for index, (_, width, header, _) in enumerate(windows):
        if header:
            stages[index][pl.ds(2 * SLOTS * BLOCK, HEADER)] = jnp.full(
                (HEADER, width), values[index].astype(jnp.float32)
            ).astype(stages[index].dtype)
        for c in waits[index]:
            c.wait()
        sends.append(pltpu.make_async_copy(stages[index], messages[index], sem.at[index * 5 + 4]))
        sends[-1].start()
    for c in sends:
        c.wait()


def pack(name, blocks, windows, starts, ends, q, k, v, g, *after):
    shapes = tuple(
        jax.ShapeDtypeStruct((2 * SLOTS * BLOCK + (HEADER if header else 0), width), q.dtype)
        for _, width, header, _ in windows
    )
    return pl.pallas_call(
        functools.partial(pack_kernel, blocks, windows),
        out_shape=shapes,
        in_specs=[SMEM] * 2 + [ANY] * (4 + len(after)),
        out_specs=(ANY,) * len(shapes),
        scratch_shapes=[pltpu.VMEM(shape.shape, q.dtype) for shape in shapes]
        + [pltpu.SemaphoreType.DMA((5 * len(shapes),))],
        compiler_params=pltpu.CompilerParams(vmem_limit_bytes=PACK_LIMIT),
        cost_estimate=pl.CostEstimate(
            flops=0, transcendentals=0, bytes_accessed=sum(4 * math.prod(shape.shape) for shape in shapes)
        ),
        name=name,
    )(starts, ends, q, k, v, g, *after)


def attend_pairs(count, head_dim, pairs, q_row, k_row, kb, vb, qb, gb, dk, dv, ob, dqb):
    dtype = kb.dtype
    scale = 1.0 / math.sqrt(head_dim)
    window = pl.ds(k_row, count * BLOCK)
    block = pl.ds(q_row, BLOCK)
    left = lax.broadcasted_iota(jnp.int32, (BLOCK, 2 * head_dim), 1) < head_dim
    zero = jnp.zeros((BLOCK, 2 * head_dim), dtype)
    by_row = (((1,), (1,)), ((), ()))
    by_key = (((0,), (0,)), ((), ()))
    plain = (((1,), (0,)), ((), ()))
    dot = functools.partial(lax.dot_general, preferred_element_type=jnp.float32)

    def split(x):
        return jnp.concatenate([jnp.where(left, x, zero), jnp.where(left, zero, x)], axis=0)

    def diagonal(x):
        return jnp.concatenate([x[:head_dim, :BLOCK], x[head_dim:, BLOCK:]], axis=0).T.astype(dtype)

    fronts = []
    for pair in range(pairs):
        lanes = pl.ds(pair * 2 * head_dim, 2 * head_dim)
        q = split(qb[block, lanes] * jnp.asarray(scale, dtype))
        g = split(gb[block, lanes])
        keys, values = kb[window, lanes], vb[window, lanes]
        fronts.append((lanes, q, g, keys, values, dot(keys, q, by_row), dot(values, g, by_row)))
    middles = []
    for lanes, q, g, keys, values, scores, grad_probs in fronts:
        weights = jnp.exp(scores - jnp.max(scores, axis=0, keepdims=True))
        total = 1.0 / jnp.sum(weights, axis=0, keepdims=True)
        row_dot = jnp.sum(weights * grad_probs, axis=0, keepdims=True) * total
        probs = weights * total
        middles.append((probs.astype(dtype), (probs * (grad_probs - row_dot)).astype(dtype)))
    for (lanes, q, g, keys, values, _, _), (probs, grad_scores) in zip(fronts, middles):
        out = dot(values, probs, by_key)
        grad_q = dot(keys, grad_scores, by_key) * scale
        add_v = dot(probs, g, plain)
        add_k = dot(grad_scores, q, plain)
        ob[block, lanes] = diagonal(out)
        dqb[block, lanes] = diagonal(grad_q)
        dv[window, lanes] += add_v
        dk[window, lanes] += add_k


def attend_kernel(
    blocks, low_col, width, inter_row, intra_col, forward_col, head_dim,
    starts, ends, q, k, v, g, inter, intra, inter_head, intra_head, *rest
):
    attended, grad_q, back_intra, back_inter, grad_k, grad_v = rest[-18:-12]
    kb, vb, qb, gb, dk, dv, ob, dqb, low, head, ahead, sem = rest[-12:]
    first, is_odd = position(blocks)
    cols = pl.ds(low_col, width)
    own = rows(SLOTS, blocks)
    make = pltpu.make_async_copy
    note = pl.ds(2 * SLOTS * BLOCK, HEADER)
    heads = [
        make(inter_head.at[note, pl.ds(0, BLOCK)], head.at[0], sem.at[0]),
        make(intra_head.at[note, pl.ds(0, BLOCK)], head.at[1], sem.at[1]),
    ]
    loads = [
        make(k.at[:, cols], kb.at[own], sem.at[2]),
        make(v.at[:, cols], vb.at[own], sem.at[3]),
        make(q.at[:, cols], qb.at[rows(1, blocks)], sem.at[4]),
        make(g.at[:, cols], gb.at[rows(1, blocks)], sem.at[5]),
    ]
    for c in heads + loads:
        c.start()
    for c in heads:
        c.wait()
    up = moved_up(starts, ends, first, blocks)
    down = moved_down(starts, ends, first)
    onward = []
    if forward_col is not None:
        onward = gather(
            edge(blocks, is_odd, up, down), pl.ds(forward_col, width), q, k, v, g, ahead, lambda i: sem.at[14 + i]
        )
    from_inter = jnp.max(head[0].astype(jnp.float32)).astype(jnp.int32)
    from_intra = jnp.max(head[1].astype(jnp.float32)).astype(jnp.int32)
    below_span = jnp.where(is_odd, from_intra, from_inter)
    above_span = jnp.where(is_odd, from_inter, from_intra)

    near_below, far_below = SLOTS - 1, SLOTS - 2
    near_above, far_above = SLOTS + blocks, SLOTS + blocks + 1
    base = 6

    def arrive(message, near, far, target, span, slot):
        at = lambda i: sem.at[base + slot * 4 + i]
        always = [make(message(0), kb.at[rows(near)], at(0)), make(message(1), vb.at[rows(near)], at(1))]
        moved = [make(message(2), qb.at[rows(target)], at(2)), make(message(3), gb.at[rows(target)], at(3))]
        stays = [make(message(2), kb.at[rows(far)], at(2)), make(message(3), vb.at[rows(far)], at(3))]
        for c in always:
            c.start()

        @pl.when(span > 0)
        def _():
            for c in moved:
                c.start()

        @pl.when(span == 0)
        def _():
            for c in stays:
                c.start()

        return always + stays

    inter_near = jnp.where(is_odd, near_above, near_below)
    inter_far = jnp.where(is_odd, far_above, far_below)
    inter_target = jnp.where(is_odd, blocks + 1, 0)
    intra_near = jnp.where(is_odd, near_below, near_above)
    intra_far = jnp.where(is_odd, far_below, far_above)
    intra_target = jnp.where(is_odd, 0, blocks + 1)
    loads += arrive(lambda i: inter.at[pl.ds(inter_row + i * BLOCK, BLOCK)], inter_near, inter_far, inter_target, from_inter, 0)
    columns = pl.ds(intra_col, width)
    loads += arrive(lambda i: intra.at[rows(i), columns], intra_near, intra_far, intra_target, from_intra, 1)
    dk[...] = jnp.zeros_like(dk)
    dv[...] = jnp.zeros_like(dv)
    for c in loads:
        c.wait()
    back = pl.ds(0, 2 * SLOTS * BLOCK)
    for c in onward:
        c.wait()
    if onward:
        onward = [make(ahead, back_inter.at[pl.ds(2 * SLOTS * BLOCK, 2 * SLOTS * BLOCK)], sem.at[14])]
        onward[0].start()

    def task(index, carry):
        mine = jnp.clip(index - 1, 0, blocks - 1)
        lower, upper = index == 0, index == blocks + 1
        span = ends[mine] - starts[mine]
        gone = ((index == 1) & down) | ((index == blocks) & up)
        span = jnp.where(gone, 0, span)
        span = jnp.where(lower, below_span, jnp.where(upper, above_span, span))
        window = starts[mine] - first + SLOTS
        window = jnp.where(lower, near_below, jnp.where(upper, near_above - REACH, window))
        q_row = pl.multiple_of(index * BLOCK, BLOCK)
        k_row = pl.multiple_of(window * BLOCK, BLOCK)
        for size in range(1, MAX_BAND + 1):

            @pl.when(span == size)
            def _():
                attend_pairs(
                    size, head_dim, width // (2 * head_dim), q_row, k_row, kb, vb, qb, gb, dk, dv, ob, dqb
                )

        return carry

    lax.fori_loop(0, blocks + 2, task, 0)

    def leave(target, near, far, block, span, slot):
        low[slot, rows(0)] = dk[rows(near)].astype(low.dtype)
        low[slot, rows(1)] = dv[rows(near)].astype(low.dtype)

        @pl.when(span > 0)
        def _():
            low[slot, rows(2)] = ob[rows(block)]
            low[slot, rows(3)] = dqb[rows(block)]

        @pl.when(span == 0)
        def _():
            low[slot, rows(2)] = dk[rows(far)].astype(low.dtype)
            low[slot, rows(3)] = dv[rows(far)].astype(low.dtype)

        c = make(low.at[slot], target, sem.at[slot])
        c.start()
        return c

    stores = onward + [leave(back_inter.at[back], inter_near, inter_far, inter_target, from_inter, 0)]
    stores += [
        make(ob.at[rows(1, blocks)], attended.at[:, cols], sem.at[2]),
        make(dqb.at[rows(1, blocks)], grad_q.at[:, cols], sem.at[3]),
        make(dk.at[own], grad_k, sem.at[4]),
        make(dv.at[own], grad_v, sem.at[5]),
    ]
    for c in stores[-4:]:
        c.start()
    stores.append(leave(back_intra, intra_near, intra_far, intra_target, from_intra, 1))
    for c in stores:
        c.wait()


def attend(name, blocks, low_col, width, offsets, head_dim, starts, ends, q, k, v, g, messages, outs):
    inter_row, intra_col, forward_col = offsets
    low, high = q.dtype, jnp.float32
    message = 2 * SLOTS * BLOCK
    whole = jax.ShapeDtypeStruct(q.shape, low)
    back = jax.ShapeDtypeStruct((message, width), low)
    joint = back if forward_col is None else jax.ShapeDtypeStruct((2 * message, width), low)
    total = jax.ShapeDtypeStruct((blocks * BLOCK, width), high)
    sources, targets = (blocks + 2 * SLOTS) * BLOCK, (blocks + 2) * BLOCK
    pairs = blocks * MAX_BAND * (width // (2 * head_dim))
    return pl.pallas_call(
        functools.partial(attend_kernel, blocks, low_col, width, inter_row, intra_col, forward_col, head_dim),
        out_shape=(whole, whole, back, joint, total, total),
        in_specs=[SMEM] * 2 + [ANY] * (8 + len(outs)),
        out_specs=(ANY,) * 6,
        input_output_aliases={10 + i: i for i in range(len(outs))},
        scratch_shapes=[
            pltpu.VMEM((sources, width), low),
            pltpu.VMEM((sources, width), low),
            pltpu.VMEM((targets, width), low),
            pltpu.VMEM((targets, width), low),
            pltpu.VMEM((sources, width), high),
            pltpu.VMEM((sources, width), high),
            pltpu.VMEM((targets, width), low),
            pltpu.VMEM((targets, width), low),
            pltpu.VMEM((2, message, width), low),
            pltpu.VMEM((2, HEADER, BLOCK), low),
            pltpu.VMEM((message, width), low),
            pltpu.SemaphoreType.DMA((18,)),
        ],
        compiler_params=pltpu.CompilerParams(vmem_limit_bytes=VMEM_LIMIT),
        cost_estimate=pl.CostEstimate(
            flops=4 * pairs * 12 * BLOCK * 2 * BLOCK * BLOCK, transcendentals=pairs * 2 * BLOCK * BLOCK,
            bytes_accessed=16 * blocks * BLOCK * width,
        ),
        name=name,
    )(starts, ends, q, k, v, g, *messages, *outs)


def settle_kernel(blocks, parts, starts, ends, *refs):
    count = len(parts)
    totals, messages = refs[: 2 * count], refs[2 * count : 3 * count]
    attended, grad_q, out_k, out_v = refs[-3 * count - 5 : -3 * count - 1]
    landed, sums = refs[-3 * count - 1 : -2 * count - 1], refs[-2 * count - 1 : -count - 1]
    stages, sem = refs[-count - 1 : -1], refs[-1]
    first, is_odd = position(blocks)
    up = moved_up(starts, ends, first, blocks)
    down = moved_down(starts, ends, first)
    make = pltpu.make_async_copy
    sides = [edge(blocks, jnp.logical_not(is_odd) if intra else is_odd, up, down) for _, _, intra in parts]
    loads = []
    for i in range(count):
        near, far, _ = sides[i]
        loads.append([
            make(messages[i].at[pl.ds(0, 2 * SLOTS * BLOCK)], landed[i], sem.at[i, 0]),
            make(totals[2 * i].at[rows(near)], sums[i].at[rows(0)], sem.at[i, 1]),
            make(totals[2 * i + 1].at[rows(near)], sums[i].at[rows(1)], sem.at[i, 2]),
            make(totals[2 * i].at[rows(far)], sums[i].at[rows(2)], sem.at[i, 3]),
            make(totals[2 * i + 1].at[rows(far)], sums[i].at[rows(3)], sem.at[i, 4]),
        ])
        for c in loads[-1]:
            c.start()
    stores, finished = [], []
    for i, (low_col, width, _) in enumerate(parts):
        cols = pl.ds(low_col, width)
        near, far, moved = sides[i]
        keep = jnp.logical_not(moved)
        for c in loads[i]:
            c.wait()
        for half in range(2):
            came = landed[i][rows(2 * half, 2)].astype(jnp.float32)
            if half:
                came = jnp.where(keep, came, jnp.zeros_like(came))
            stages[i][rows(2 * half, 2)] = (sums[i][rows(2 * half, 2)] + came).astype(stages[i].dtype)
            block = far if half else near
            stores += [
                make(stages[i].at[rows(2 * half)], out_k.at[rows(block), cols], sem.at[i, 2 * half]),
                make(stages[i].at[rows(2 * half + 1)], out_v.at[rows(block), cols], sem.at[i, 2 * half + 1]),
            ]
            for c in stores[-2:]:
                c.start()

        whole = [
            make(landed[i].at[rows(2)], attended.at[rows(near), cols], sem.at[i, 4]),
            make(landed[i].at[rows(3)], grad_q.at[rows(near), cols], sem.at[i, 5]),
        ]
        finished.append((moved, whole))

        @pl.when(moved)
        def _():
            for c in whole:
                c.start()

    for moved, whole in finished:

        @pl.when(moved)
        def _():
            for c in whole:
                c.wait()

    for c in stores:
        c.wait()


def settle(name, blocks, parts, starts, ends, totals, messages, outs):
    low = outs[0].dtype
    whole = jax.ShapeDtypeStruct(outs[0].shape, low)
    count = len(parts)
    shapes = [(2 * SLOTS * BLOCK, width) for _, width, _ in parts]
    base = 2 + 3 * count
    return pl.pallas_call(
        functools.partial(settle_kernel, blocks, parts),
        out_shape=(whole,) * 4,
        in_specs=[SMEM] * 2 + [ANY] * (3 * count + len(outs)),
        out_specs=(ANY,) * 4,
        input_output_aliases={base + i: i for i in range(len(outs))},
        scratch_shapes=[pltpu.VMEM(shape, low) for shape in shapes]
        + [pltpu.VMEM(shape, jnp.float32) for shape in shapes]
        + [pltpu.VMEM(shape, low) for shape in shapes]
        + [pltpu.SemaphoreType.DMA((count, 6))],
        compiler_params=pltpu.CompilerParams(vmem_limit_bytes=SMALL_LIMIT),
        cost_estimate=pl.CostEstimate(
            flops=0, transcendentals=0, bytes_accessed=sum(SETTLE_WEIGHT * math.prod(shape) for shape in shapes)
        ),
        name=name,
    )(starts, ends, *totals, *messages, *outs)


def body(q, k, v, g, starts, ends):
    shard_rows, model_width = q.shape
    blocks = shard_rows // BLOCK
    head_dim = model_width // H
    count = lax.axis_size("seq")
    across = [(i, i + 1) for i in range(1, count - 1, 2)] + [(i + 1, i) for i in range(1, count - 1, 2)]
    inside = [(i, i ^ 1) for i in range(count)]
    pieces, low_col = [], 0
    for pairs in PIECES:
        pieces.append((low_col, pairs * 2 * head_dim))
        low_col += pairs * 2 * head_dim

    first, last = pieces[0], len(pieces) - 1
    rest_col = first[1]
    swap = lambda x, pairs: lax.ppermute(x, "seq", pairs)
    inter, intra = pack("pack0", blocks, [(*first, True, False), (*first, True, True)], starts, ends, q, k, v, g)
    heads = (swap(inter, across), swap(intra, inside))
    inter, intra = pack(
        "pack1", blocks, [(*pieces[1], False, False), (rest_col, model_width - rest_col, False, True)],
        starts, ends, q, k, v, g, inter,
    )
    arrived = [heads, (swap(inter, across), swap(intra, inside))]

    outs, totals, returned = (), [], []
    for i, piece in enumerate(pieces):
        if i > 1:
            arrived.append((returned[i - 2][0], arrived[1][1]))
        inter_row = 2 * SLOTS * BLOCK if i > 1 else 0
        intra_col = piece[0] - rest_col if i else 0
        forward_col = pieces[i + 2][0] if i + 2 <= last else None
        results = attend(
            f"attend{i}", blocks, *piece, (inter_row, intra_col, forward_col), head_dim, starts, ends, q, k, v, g,
            (*arrived[i], *heads), outs,
        )
        outs = results[:2]
        returned.append((swap(results[3], across), swap(results[2], inside)))
        totals.append(results[4:])
    stages = (
        [(0, False)] + [(i, True) for i in range(last + 1)],
        *([(i, False)] for i in range(1, last + 1)),
    )
    for stage, members in enumerate(stages):
        parts = [(*pieces[i], inner) for i, inner in members]
        outs = settle(
            f"settle{stage}", blocks, parts, starts, ends, [x for i, _ in members for x in totals[i]],
            [returned[i][int(inner)] for i, inner in members], outs,
        )
    return outs


def solution(mesh):
    spec = P(("groups", "seq"), None)
    flat = P(("groups", "seq"))
    return jax.shard_map(
        body,
        mesh=mesh,
        in_specs=(spec, spec, spec, spec, flat, flat),
        out_specs=(spec, spec, spec, spec),
        check_vma=False,
    )
```
